32 devices in a mesh: perm: 2 (over y), subj: 8 (over z, core), vert: 2 (over x).
Axes of the slice: x: 2, y: 2, z: 4, core: 2. Of those that a mesh axis runs over, the one named last changes fastest.
Arguments:
- kinship: bfloat16 [2048, 2048], P('subj')
- phenotype: bfloat16 [2048, 2048], P('subj', 'vert')
- shuffle: int32 [4096], P(('perm', 'subj')), parts along dimension 0, may hold values from 0 to 2047, as said below
Outputs:
- statistic: float32 [4096], P(('perm', 'vert')), parts along dimension 0
The draws below stay inside these ranges and needn't reach their ends.
There are 2 independent parts, one for each index of `perm`. The reference program is written for one: setup_inputs(seed, part) draws one part's arguments, and reference() takes and returns one part's arrays. A program takes and returns all parts, laid end to end along the dimension named above; an argument that names none is the same for every part. Nothing has to cross between parts.
Inputs may be any that keep to these rules, and one draw needn't show every extreme that they name: shuffle is a permutation of 0 to 2047 that maps every subject into its own exchangeability block.
All inputs are finite; a program needn't handle non-finite values.
Results may differ from the reference program's by a relative error of at most 0.0003.
Values may be sent and summed in bfloat16 or wider, within the bound.
A program may use at most 128 MiB of HBM per device.

```python
import jax
import jax.numpy as jnp
from jax import lax

BLOCKS = 16
SUBJECTS = 2048
VERTICES = 2048


def draw_kinship(key, part):
    key_noise, key_diag = jax.random.split(key)
    entries = jax.random.normal(key_noise, (SUBJECTS, SUBJECTS), jnp.float32)
    symmetric = 0.4 * (entries + entries.T) / jnp.sqrt(2.0 * SUBJECTS)
    diagonal = 0.8 + 0.4 * jax.random.uniform(key_diag, (SUBJECTS,), jnp.float32)
    identity = jnp.eye(SUBJECTS, dtype=jnp.float32)
    return (symmetric * (1.0 - identity) + identity * diagonal[:, None]).astype(jnp.bfloat16)


def draw_phenotype(key, part):
    key_noise, key_rows, key_cols = jax.random.split(key, 3)
    entries = jax.random.normal(key_noise, (SUBJECTS, VERTICES), jnp.float32)
    position = jnp.arange(SUBJECTS, dtype=jnp.float32) / SUBJECTS
    row_scale = jnp.exp(1.0986123 * position + 2.3025851 * jax.random.uniform(key_rows, (SUBJECTS,), jnp.float32)) / 4.0
    col_scale = jnp.exp(2.3025851 * jax.random.uniform(key_cols, (VERTICES,), jnp.float32)) / 3.0
    return (entries * row_scale[:, None] * col_scale[None, :]).astype(jnp.bfloat16)


def draw_shuffle(key, part):
    key_block, key_rank = jax.random.split(key)
    block_ids = jax.random.randint(key_block, (SUBJECTS,), 0, BLOCKS).astype(jnp.int32)
    ranks = jax.random.permutation(key_rank, SUBJECTS).astype(jnp.int32)
    positions = jnp.arange(SUBJECTS, dtype=jnp.int32)
    source_order = jnp.argsort(block_ids * SUBJECTS + ranks, stable=True).astype(jnp.int32)
    target_order = jnp.argsort(block_ids * SUBJECTS + positions, stable=True).astype(jnp.int32)
    return jnp.zeros((SUBJECTS,), jnp.int32).at[target_order].set(source_order)


def setup_inputs(seed: int = 0, part: int = 0) -> dict:
    streams_of = jax.random.split(jax.random.key(seed), 4)
    part_splits = jax.random.split(jax.random.fold_in(streams_of[3], part), 4)
    kinship = draw_kinship(jax.random.fold_in(streams_of[3], 71), part)
    phenotype = draw_phenotype(jax.random.fold_in(streams_of[3], 71), part)
    shuffle = draw_shuffle(jax.random.fold_in(jax.random.fold_in(streams_of[3], part), 71), part)
    return dict(kinship=kinship, phenotype=phenotype, shuffle=shuffle)


def reference(kinship, phenotype, shuffle):
    permuted = jnp.take(phenotype, shuffle.astype(jnp.int32), axis=0)
    product = jnp.dot(kinship, permuted, preferred_element_type=jnp.float32)
    kin_diag = jnp.diagonal(kinship).astype(jnp.float32)
    moved = permuted.astype(jnp.float32)
    cross_term = lax.optimization_barrier(jnp.sum(moved * (product - kin_diag[:, None] * moved), axis=0))
    values = phenotype.astype(jnp.float32)
    squares = lax.optimization_barrier(jnp.sum(values * values, axis=0))
    subject_count = kinship.shape[0]
    return cross_term / (jnp.sqrt(jnp.float32(subject_count)) * (squares / subject_count + 1e-05))
```

```python
import functools

import jax
import jax.numpy as jnp
from jax import lax
from jax.experimental import pallas as pl
from jax.experimental.pallas import tpu as pltpu
from jax.sharding import PartitionSpec as P

MESH = pl.DeviceIdType.MESH
CORES = 2
PIECES = 4
SHARED = 3
SPAN = 4


def kernel(
    n_perm, n_subj, n_vert,
    kin_hbm, phe_hbm, shf_hbm, out_ref,
    kin, end_kin, kin_t, end_t, shuf, moved, gathered, acc, parts, final,
    load_sem, up, peers, lines,
    shuf_recv, shuf_own, shuf_in,
    row_recv, own_send, row_send, sib_send,
    end_recv, end_send, end_share, fin_send, fin_recv,
):
    perm, subj, vert = lax.axis_index("perm"), lax.axis_index("subj"), lax.axis_index("vert")
    n_all = n_perm * n_subj
    me = perm * n_subj + subj
    z, core = subj // CORES, lax.rem(subj, CORES)
    n_z = n_subj // CORES
    last = n_z - 1
    sibling = z * CORES + (1 - core)
    rows, cols = kin.shape[0], gathered.shape[2]
    piece = rows // PIECES
    n_list = kin.shape[1] // rows
    n_spans = gathered.shape[0] // SPAN
    n_plane = n_perm * CORES
    n_in = n_vert * n_plane
    n_chips = n_vert * n_perm
    chip = vert * n_perm + perm
    share = rows // n_chips
    place = chip * CORES + core
    inner = jnp.logical_and(z > 0, z < last)
    by_end = jnp.logical_or(z == 1, z == last - 1)
    first_col = pl.multiple_of(perm * cols, cols)
    barrier = pltpu.get_barrier_semaphore()

    def signal(sem, **device):
        pl.semaphore_signal(sem, inc=1, device_id=device, device_id_type=MESH)

    def in_plane(t):
        return dict(vert=t // n_plane, perm=lax.rem(t // CORES, n_perm), subj=z * CORES + lax.rem(t, CORES))

    def half(h):
        return pl.ds(pl.multiple_of(h * piece, piece), piece)

    def spot(q, c, h):
        at = pl.multiple_of(lax.rem(h, 2) * (2 * piece) + c * piece, piece)
        return gathered.at[q * 2 + h // 2, pl.ds(at, piece)]

    near = jnp.where(z * 2 < n_z, 0, last)
    far = last - near
    low_end = near == 0
    far_core = jnp.where(low_end, core, 1 - core)

    def listed(l):
        if l == 0:
            return near * CORES + core
        if l == 1:
            return near * CORES + 1 - core
        if l == 2:
            return far * CORES + far_core
        if l == 3:
            return far * CORES + 1 - far_core
        if l == 4:
            return subj
        if l == 5:
            return sibling
        k = l - 5
        other = jnp.where(k < z, k, k + 1)
        return other * CORES + jnp.where(other > z, core, 1 - core)

    def kin_load(l):
        block = pl.multiple_of(listed(l) * rows, rows)
        return pltpu.make_async_copy(
            kin_hbm.at[:, pl.ds(block, rows)], kin.at[:, l * rows:(l + 1) * rows], load_sem.at[PIECES + l])

    def phe_load(h):
        return pltpu.make_async_copy(
            phe_hbm.at[half(h), pl.ds(first_col, cols)], spot(z, core, h), load_sem.at[h])

    loads = [functools.partial(kin_load, l) for l in range(n_list)]
    loads += [functools.partial(phe_load, h) for h in range(PIECES)]

    @pl.loop(z + 1, n_z)
    def _(q):
        signal(barrier, subj=q * CORES + core)

    @pl.loop(place + 1, n_in)
    def _(t):
        signal(barrier, **in_plane(t))

    @pl.when(z + place > 0)
    def _():
        pl.semaphore_wait(barrier, z + place)

    @pl.loop(1, z + 1)
    def _(d):
        signal(up.at[d], subj=subj - CORES * d)

    @pl.loop(0, place)
    def _(t):
        signal(peers, **in_plane(t))

    def remote(src, dst, send, recv, **device):
        return pltpu.make_async_remote_copy(
            src_ref=src, dst_ref=dst, send_sem=send, recv_sem=recv, device_id=device, device_id_type=MESH)

    def own_copy(h, way, target):
        return remote(
            phe_hbm.at[half(h), pl.ds(first_col, cols)], spot(z, core, h),
            own_send.at[way, h], row_recv.at[subj, h], subj=target)

    def pass_copy(slot, h, sems, target):
        here = spot(slot // CORES, lax.rem(slot, CORES), h)
        return remote(here, here, sems.at[slot, h], row_recv.at[slot, h], subj=target)

    def shuf_own_copy(q):
        return remote(shf_hbm, shuf.at[me], shuf_own.at[q], shuf_recv.at[me], subj=q * CORES + core)

    def shuf_wait(slot):
        remote(shuf.at[slot], shuf.at[slot], shuf_own.at[0], shuf_recv.at[slot], subj=sibling).wait_recv()

    def shuf_in_copy(src, slot, k):
        t = lax.rem(perm * CORES + core + k, n_plane)
        line = slot - perm * n_subj
        return remote(src, shuf.at[slot], shuf_in.at[line, k], shuf_recv.at[slot],
                      perm=t // CORES, subj=z * CORES + lax.rem(t, CORES))

    def part_of(owner):
        return pl.ds(pl.multiple_of(owner * share, share), share)

    def end_block(i):
        end_core = core if i == 0 else 1 - core
        if i < 2:
            return z * CORES + end_core
        return jnp.where(z == 0, last * CORES + core, 1 - core)

    def end_copy(i, target):
        block = pl.multiple_of(end_block(i) * rows, rows)
        return remote(
            kin_hbm.at[part_of(chip), pl.ds(block, rows)], end_kin.at[part_of(chip), i * rows:(i + 1) * rows],
            end_send.at[i], end_recv.at[chip, i], subj=target)

    def end_share_copy(i, owner, t):
        here = end_kin.at[part_of(owner), i * rows:(i + 1) * rows]
        return remote(here, here, end_share.at[i, t], end_recv.at[owner, i], vert=t // n_perm, perm=lax.rem(t, n_perm))

    def send_ends(target, act):
        @pl.when(jnp.logical_not(inner))
        def _():
            for i in range(SHARED):
                act(end_copy(i, target))

    def send_rows(way, target, act):
        for h in range(PIECES):
            act(own_copy(h, way, target))

    def start(copy):
        copy.start()

    def finish(copy):
        copy.wait_send()

    to_low, to_high = z >= 2, z <= last - 2

    @pl.when(to_low)
    def _():
        @pl.loop(1, z)
        def _(k):
            shuf_own_copy(z - k).start()

        send_ends(subj - CORES, start)
        send_rows(0, subj - CORES, start)

    @pl.when(inner)
    def _():
        for load in loads:
            load().start()

    @pl.when(to_high)
    def _():
        pl.semaphore_wait(up.at[1], 1)
        shuf_own_copy(z + 1).start()
        send_ends(subj + CORES, start)

        @pl.loop(2, last - z)
        def _(d):
            pl.semaphore_wait(up.at[d], 1)
            shuf_own_copy(z + d).start()

        send_rows(1, subj + CORES, start)

    @pl.when(place < n_in - 1)
    def _():
        pl.semaphore_wait(peers, n_in - 1 - place)

    def event(dist, h, act):
        @pl.when(z + dist < n_z)
        def _():
            act(subj + CORES * dist, h, z > 1, subj - CORES)

        @pl.when(z - dist >= 0)
        def _():
            act(subj - CORES * dist, h, z < last - 1, subj + CORES)

    def arrive(slot, h, onward, target):
        pass_copy(slot, h, row_send, sibling).wait_recv()

        @pl.when(onward)
        def _():
            pass_copy(slot, h, row_send, target).start()

        pass_copy(slot, h, sib_send, sibling).start()

    def drain(slot, h, onward, target):
        @pl.when(onward)
        def _():
            pass_copy(slot, h, row_send, target).wait_send()

        pass_copy(slot, h, sib_send, sibling).wait_send()

    def shuf_arrive(subj_slot, h, onward, target):
        slot = perm * n_subj + subj_slot
        shuf_wait(slot)
        for k in range(1, n_plane):
            shuf_in_copy(shuf.at[slot], slot, k).start()

    def shuf_drain(subj_slot, h, onward, target):
        slot = perm * n_subj + subj_slot
        for k in range(1, n_plane):
            shuf_in_copy(shuf.at[slot], slot, k).wait_send()

    span = SPAN * rows
    spot_row = lax.broadcasted_iota(jnp.int32, (span, rows), 0)
    spot_id = (
        spot_row // (2 * piece) * piece // rows * (CORES * rows) + lax.rem(spot_row // (2 * piece) * piece, rows)
        + lax.rem(spot_row // piece, 2) * rows + lax.rem(spot_row, piece))

    def picks_of(p, turn, l):
        ids = spot_id + turn * span
        return (ids == shuf[p * n_subj + listed(l)]).astype(jnp.bfloat16)

    def move_own(task):
        p, turn = task // n_spans, lax.rem(task, n_spans)
        picks = [picks_of(p, turn, l) for l in range(n_list)]
        out = jnp.dot(jnp.concatenate(picks, axis=1), kin_t[...], preferred_element_type=jnp.float32)
        at = pl.ds(pl.multiple_of(turn * span, span), span)
        moved[2 * p, at] = out.astype(jnp.bfloat16)
        moved[2 * p + 1, at] = picks[4]
        moved[2 * (n_perm + p) + 1, at] = picks[0]

    def move_end(task):
        p, turn = task // n_spans, lax.rem(task, n_spans)
        picks = [picks_of(p, turn, l) for l in range(SHARED)]
        out = jnp.dot(jnp.concatenate(picks, axis=1), end_t[...], preferred_element_type=jnp.float32)
        at = pl.ds(pl.multiple_of(turn * span, span), span)
        moved[2 * (n_perm + p), at] = out.astype(jnp.bfloat16)

    n_half = n_perm * 2

    def add(chunks, part, first=False):
        for q in range(part * n_half, (part + 1) * n_half):
            total = None if first else acc[q]
            for chunk in chunks:
                at = pl.ds(pl.multiple_of(chunk * rows, rows), rows)
                term = lax.dot_general(
                    moved[q, at], gathered[chunk], (((0,), (0,)), ((), ())), preferred_element_type=jnp.float32)
                total = term if total is None else total + term
            acc[q] = total

    def sides(dist, act):
        @pl.loop(0, 2)
        def _(side):
            q = z + dist * (1 - 2 * side)

            @pl.when(jnp.logical_and(q >= 0, q < n_z))
            def _():
                act(q)

    def await_sibling(q, hs):
        for h in hs:
            pass_copy(q * CORES + 1 - core, h, row_send, sibling).wait_recv()

    def turn_block(src, dst, l, scale, clear=False):
        block = jnp.transpose(src[:, l * rows:(l + 1) * rows].astype(jnp.float32)) * scale
        if clear:
            down = lax.broadcasted_iota(jnp.int32, (rows, rows), 0)
            across = lax.broadcasted_iota(jnp.int32, (rows, rows), 1)
            block = jnp.where(down == across, 0.0, block)
        dst[l * rows:(l + 1) * rows] = block.astype(jnp.bfloat16)

    def square_sum(chunk):
        own = gathered[chunk].astype(jnp.float32)
        return jnp.sum(own * own, axis=0, keepdims=True)

    n_tasks = n_perm * n_spans
    turns = PIECES

    per_hub = n_subj - 2 * CORES

    def hub_slot(p, s):
        return p * per_hub + s - CORES

    per_z = n_all // n_z

    def fin_copy(k):
        to_z, rest = k // per_z, lax.rem(k, per_z)
        to_perm, to_subj = rest // CORES, to_z * CORES + lax.rem(rest, CORES)
        mine = hub_slot(perm, subj)
        copy = remote(parts.at[to_perm], final.at[mine], fin_send.at[k], fin_recv.at[mine],
                      perm=to_perm, subj=to_subj)
        return copy, to_perm * n_subj + to_subj != me

    @pl.when(inner)
    def _():
        for k in range(1, n_plane):
            shuf_in_copy(shf_hbm, me, k).start()
        for h in range(PIECES):
            own_copy(h, 2, sibling).start()
        own_shuf = pltpu.make_async_copy(shf_hbm, shuf.at[me], load_sem.at[PIECES + n_list])
        own_shuf.start()
        own_shuf.wait()
        for load in loads:
            load().wait()
        for l in range(n_list):
            turn_block(kin, kin_t, l, 0.5 if l in (4, 5) else 1.0, clear=l == 4)

        @pl.loop(1, last)
        def _(dist):
            event(dist, 0, shuf_arrive)

        @pl.when(by_end)
        def _():
            for i in range(SHARED):
                end_share_copy(i, chip, chip).wait_recv()
                for k in range(1, n_chips):
                    end_share_copy(i, chip, lax.rem(chip + k, n_chips)).start()

        @pl.loop(jnp.where(to_high, last - z, 1), n_z - z)
        def _(d):
            pl.semaphore_wait(up.at[d], 1)

        for k in range(1, n_plane):
            t = lax.rem(perm * CORES + core + k, n_plane)
            signal(lines, perm=t // CORES, subj=z * CORES + lax.rem(t, CORES))

        @pl.loop(1, n_plane)
        def _(k):
            t = lax.rem(perm * CORES + core + k, n_plane)

            @pl.loop(0, n_z)
            def _(q):
                slot = (t // CORES) * n_subj + q * CORES + lax.rem(t, CORES)
                shuf_wait(slot)

        @pl.loop(0, turns)
        def _(turn):
            event(1, turn, arrive)

            @pl.loop(turn * n_tasks // turns, (turn + 1) * n_tasks // turns)
            def _(task):
                move_own(task)

        await_sibling(z, range(PIECES))
        parts[0, 1:2] = square_sum(z * 2 + core)
        add([z * 2, z * 2 + 1], 0, first=True)
        event(2, 0, arrive)

        def add_own(q):
            await_sibling(q, range(PIECES))
            add([q * 2, q * 2 + 1], 0)

        sides(1, add_own)
        event(2, 1, arrive)

        @pl.when(by_end)
        def _():
            @pl.loop(1, n_chips)
            def _(k):
                for i in range(SHARED):
                    end_share_copy(i, lax.rem(chip + k, n_chips), chip).wait_recv()

            for l in range(SHARED):
                turn_block(end_kin, end_t, l, 0.5 if l < 2 else 1.0, clear=l == 0)
            parts[0, 1:2] += square_sum(near * 2 + core)

        @pl.when(jnp.logical_not(by_end))
        def _():
            end_t[...] = jnp.zeros_like(end_t)

        for p in range(1, n_perm):
            parts[p, 1:2] = parts[0, 1:2]

        @pl.loop(0, 2)
        def _(turn):
            @pl.loop(turn * n_tasks // 2, (turn + 1) * n_tasks // 2)
            def _(task):
                move_end(task)

            event(2, 2 + turn, arrive)

        add([z * 2, z * 2 + 1], 1, first=True)
        sides(1, lambda q: add([q * 2, q * 2 + 1], 1))

        def add_all(q):
            for j in range(2):
                await_sibling(q, range(2 * j, 2 * j + 2))
                for part in range(2):
                    add([q * 2 + j], part)

        sides(2, add_all)
        if last > 3:
            @pl.loop(3, last)
            def _(dist):
                for h in range(PIECES):
                    event(dist, h, arrive)
                sides(dist, add_all)

        for p in range(n_perm):
            cross = 0.0
            for part in range(2):
                at = (part * n_perm + p) * 2
                cross += jnp.sum(acc[at] * acc[at + 1], axis=0, keepdims=True)
            parts[p, 0:1] = cross

        pl.semaphore_wait(lines, n_plane - 1)

        @pl.loop(0, n_all)
        def _(k):
            copy, other = fin_copy(k)
            pl.when(other)(copy.start)

        final[hub_slot(perm, subj)] = parts[perm]

    @pl.loop(0, n_perm)
    def _(p):
        @pl.loop(CORES, n_subj - CORES)
        def _(s):
            @pl.when(p * n_subj + s != me)
            def _():
                slot = hub_slot(p, s)
                remote(parts.at[0], final.at[slot], fin_send.at[0], fin_recv.at[slot], subj=sibling).wait_recv()

    count = n_subj * rows
    for q in range(n_perm):
        total = jnp.sum(final[q * per_hub:(q + 1) * per_hub], axis=0)
        scale = jnp.sqrt(jnp.float32(count)) * (total[1:2] / count + 1e-05)
        out_ref[:, q * cols:(q + 1) * cols] = 2.0 * total[0:1] / scale

    @pl.when(to_low)
    def _():
        @pl.loop(1, z)
        def _(k):
            shuf_own_copy(z - k).wait_send()

        send_ends(subj - CORES, finish)
        send_rows(0, subj - CORES, finish)

    @pl.when(to_high)
    def _():
        @pl.loop(1, last - z)
        def _(d):
            shuf_own_copy(z + d).wait_send()

        send_ends(subj + CORES, finish)
        send_rows(1, subj + CORES, finish)

    @pl.when(z == 0)
    def _():
        pl.semaphore_wait(up.at[last], 1)

    @pl.when(inner)
    def _():
        for k in range(1, n_plane):
            shuf_in_copy(shf_hbm, me, k).wait_send()
        for h in range(PIECES):
            own_copy(h, 2, sibling).wait_send()

        @pl.loop(1, last)
        def _(dist):
            event(dist, 0, shuf_drain)
            for h in range(PIECES):
                event(dist, h, drain)

        @pl.when(by_end)
        def _():
            for i in range(SHARED):
                for k in range(1, n_chips):
                    end_share_copy(i, chip, lax.rem(chip + k, n_chips)).wait_send()

        @pl.loop(0, n_all)
        def _(k):
            copy, other = fin_copy(k)
            pl.when(other)(copy.wait_send)


def per_device(n_perm, n_subj, n_vert, kinship, phenotype, shuffle):
    rows, width = phenotype.shape
    cols = width // n_perm
    n_all = n_perm * n_subj
    n_z = n_subj // CORES
    n_list = n_z + 3
    n_chips = n_vert * n_perm
    n_hubs = n_perm * (n_subj - 2 * CORES)
    DMA, VMEM = pltpu.SemaphoreType.DMA, pltpu.VMEM
    out = pl.pallas_call(
        functools.partial(kernel, n_perm, n_subj, n_vert),
        out_shape=jax.ShapeDtypeStruct((1, width), jnp.float32),
        in_specs=[pl.BlockSpec(memory_space=pl.ANY)] * 3,
        out_specs=pl.BlockSpec(memory_space=VMEM),
        scratch_shapes=[
            VMEM((rows, n_list * rows), jnp.bfloat16),
            VMEM((rows, SHARED * rows), jnp.bfloat16),
            VMEM((n_list * rows, rows), jnp.bfloat16),
            VMEM((SHARED * rows, rows), jnp.bfloat16),
            VMEM((n_all, 1, rows), jnp.int32),
            VMEM((n_perm * 4, n_subj * rows, rows), jnp.bfloat16),
            VMEM((n_z * 2, rows, cols), jnp.bfloat16),
            VMEM((n_perm * 4, rows, cols), jnp.float32),
            VMEM((n_perm, 2, cols), jnp.float32),
            VMEM((n_hubs, 2, cols), jnp.float32),
            DMA((PIECES + n_list + 1,)),
            pltpu.SemaphoreType.REGULAR((n_z,)), pltpu.SemaphoreType.REGULAR, pltpu.SemaphoreType.REGULAR,
            DMA((n_all,)), DMA((n_z,)), DMA((n_subj, n_perm * CORES)),
            DMA((n_subj, PIECES)), DMA((3, PIECES)), DMA((n_subj, PIECES)), DMA((n_subj, PIECES)),
            DMA((n_chips, SHARED)), DMA((SHARED,)), DMA((SHARED, n_chips)),
            DMA((n_all,)), DMA((n_hubs,)),
        ],
        compiler_params=pltpu.CompilerParams(collective_id=0, has_side_effects=True),
    )(kinship, phenotype, shuffle.reshape(1, rows))
    return out.reshape(width)


def solution(mesh):
    in_specs = (P("subj", None), P("subj", "vert"), P(("perm", "subj")))
    out_specs = P(("perm", "vert"))
    sizes = [mesh.shape[axis] for axis in ("perm", "subj", "vert")]
    body = functools.partial(per_device, *sizes)
    return jax.shard_map(body, mesh=mesh, in_specs=in_specs, out_specs=out_specs, check_vma=False)
```

```python
import functools

import jax
import jax.numpy as jnp
from jax import lax
from jax.experimental import pallas as pl
from jax.experimental.pallas import tpu as pltpu
from jax.sharding import PartitionSpec as P

MESH = pl.DeviceIdType.MESH
CORES = 2
PIECES = 4
SHARED = 3
SPAN = 4
END_SPAN = 4


def kernel(
    n_perm, n_subj, n_vert,
    kin_hbm, phe_hbm, shf_hbm, out_ref,
    kin, end_kin, kin_t, end_t, shuf, moved, gathered, acc, parts, final,
    load_sem, up, side, across_perm, across_vert, lines,
    shuf_recv, shuf_own, shuf_in,
    row_recv, own_send, row_send, sib_send,
    end_recv, end_send, end_share, fin_send, fin_recv,
):
    perm, subj, vert = lax.axis_index("perm"), lax.axis_index("subj"), lax.axis_index("vert")
    n_all = n_perm * n_subj
    me = perm * n_subj + subj
    z, core = subj // CORES, lax.rem(subj, CORES)
    n_z = n_subj // CORES
    last = n_z - 1
    sibling = z * CORES + (1 - core)
    rows, cols = kin.shape[0], gathered.shape[1]
    piece = rows // PIECES
    n_list = kin.shape[1] // rows
    n_spans = gathered.shape[0] // (SPAN * rows)
    n_plane = n_perm * CORES
    n_chips = n_vert * n_perm
    chip = vert * n_perm + perm
    share = rows // n_chips
    inner = jnp.logical_and(z > 0, z < last)
    by_end = jnp.logical_or(z == 1, z == last - 1)
    first_col = pl.multiple_of(perm * cols, cols)
    barrier = pltpu.get_barrier_semaphore()

    def signal(sem, **device):
        pl.semaphore_signal(sem, inc=1, device_id=device, device_id_type=MESH)

    def half(h):
        return pl.ds(pl.multiple_of(h * piece, piece), piece)

    def spot(q, c, h):
        at = pl.multiple_of((q * PIECES + h) * (CORES * piece) + c * piece, piece)
        return gathered.at[pl.ds(at, piece)]

    near = jnp.where(z * 2 < n_z, 0, last)
    far = last - near
    low_end = near == 0
    far_core = jnp.where(low_end, core, 1 - core)

    def listed(l):
        if l == 0:
            return near * CORES + core
        if l == 1:
            return near * CORES + 1 - core
        if l == 2:
            return far * CORES + far_core
        if l == 3:
            return far * CORES + 1 - far_core
        if l == 4:
            return subj
        if l == 5:
            return sibling
        k = l - 5
        other = jnp.where(k < z, k, k + 1)
        return other * CORES + jnp.where(other > z, core, 1 - core)

    def kin_load(l):
        block = pl.multiple_of(listed(l) * rows, rows)
        return pltpu.make_async_copy(
            kin_hbm.at[:, pl.ds(block, rows)], kin.at[:, l * rows:(l + 1) * rows], load_sem.at[PIECES + l])

    def phe_load(h):
        return pltpu.make_async_copy(
            phe_hbm.at[half(h), pl.ds(first_col, cols)], spot(z, core, h), load_sem.at[h])

    own_shuf = pltpu.make_async_copy(shf_hbm, shuf.at[me], load_sem.at[PIECES + n_list])
    loads = [functools.partial(kin_load, l) for l in range(n_list)]
    loads += [functools.partial(phe_load, h) for h in range(PIECES)]

    @pl.loop(z + 1, n_z)
    def _(q):
        signal(barrier, subj=q * CORES + core)

    axes = (
        (perm, n_perm, lambda d: dict(perm=perm + d)),
        (vert, n_vert, lambda d: dict(vert=vert + d)),
        (core, CORES, lambda d: dict(subj=subj + d)),
    )
    for index, size, near_by in axes:
        @pl.when(jnp.logical_and(inner, index < size - 1))
        def _():
            signal(barrier, **near_by(1))

    lower = sum((index > 0).astype(jnp.int32) for index, _, _ in axes)
    lower = z + jnp.where(inner, lower, 0)

    @pl.when(lower > 0)
    def _():
        pl.semaphore_wait(barrier, lower)

    @pl.loop(1, z + 1)
    def _(d):
        signal(up.at[d], subj=subj - CORES * d)

    def answer_plane():
        for i, (index, size, near_by) in enumerate(axes):
            @pl.when(index > 0)
            def _():
                signal(side.at[i], **near_by(-1))

    def meet(i):
        index, size, _ = axes[i]

        @pl.when(index < size - 1)
        def _():
            pl.semaphore_wait(side.at[i], 1)

    def sweep_ways(sem, i):
        index, size, near_by = axes[i]
        up_side, down_side = index < size - 1, index > 0
        return (
            (sem.at[0], lambda done: signal(done, **near_by(1)), down_side, up_side),
            (sem.at[1], lambda done: signal(done, **near_by(-1)), up_side, down_side),
        )

    def launch(sem, i):
        for done, tell, behind, ahead in sweep_ways(sem, i):
            pl.when(jnp.logical_and(ahead, jnp.logical_not(behind)))(functools.partial(tell, done))

    def finish_sweep(sem, i):
        for done, tell, behind, ahead in sweep_ways(sem, i):
            @pl.when(behind)
            def _():
                pl.semaphore_wait(done, 1)
                pl.when(ahead)(functools.partial(tell, done))

    def remote(src, dst, send, recv, **device):
        return pltpu.make_async_remote_copy(
            src_ref=src, dst_ref=dst, send_sem=send, recv_sem=recv, device_id=device, device_id_type=MESH)

    def own_copy(h, way, target):
        return remote(
            phe_hbm.at[half(h), pl.ds(first_col, cols)], spot(z, core, h),
            own_send.at[way, h], row_recv.at[subj, h], subj=target)

    def pass_copy(slot, h, sems, target):
        here = spot(slot // CORES, lax.rem(slot, CORES), h)
        return remote(here, here, sems.at[slot, h], row_recv.at[slot, h], subj=target)

    def shuf_own_copy(q):
        return remote(shf_hbm, shuf.at[me], shuf_own.at[q], shuf_recv.at[me], subj=q * CORES + core)

    def shuf_wait(slot):
        remote(shuf.at[slot], shuf.at[slot], shuf_own.at[0], shuf_recv.at[slot], subj=sibling).wait_recv()

    def shuf_in_copy(src, slot, k):
        t = lax.rem(perm * CORES + core + k, n_plane)
        line = slot - perm * n_subj
        return remote(src, shuf.at[slot], shuf_in.at[line, k], shuf_recv.at[slot],
                      perm=t // CORES, subj=z * CORES + lax.rem(t, CORES))

    def part_of(owner):
        return pl.ds(pl.multiple_of(owner * share, share), share)

    def end_block(i):
        end_core = core if i == 0 else 1 - core
        if i < 2:
            return z * CORES + end_core
        return jnp.where(z == 0, last * CORES + core, 1 - core)

    def end_copy(i, target):
        block = pl.multiple_of(end_block(i) * rows, rows)
        return remote(
            kin_hbm.at[part_of(chip), pl.ds(block, rows)], end_kin.at[part_of(chip), i * rows:(i + 1) * rows],
            end_send.at[i], end_recv.at[chip, i], subj=target)

    def end_share_copy(i, owner, t):
        here = end_kin.at[part_of(owner), i * rows:(i + 1) * rows]
        return remote(here, here, end_share.at[i, t], end_recv.at[owner, i], vert=t // n_perm, perm=lax.rem(t, n_perm))

    def send_ends(target, act):
        @pl.when(jnp.logical_not(inner))
        def _():
            for i in range(SHARED):
                act(end_copy(i, target))

    def send_rows(way, target, act):
        for h in range(PIECES):
            act(own_copy(h, way, target))

    def start(copy):
        copy.start()

    def finish(copy):
        copy.wait_send()

    to_low, to_high = z >= 2, z <= last - 2

    pl.when(inner)(answer_plane)

    @pl.when(to_low)
    def _():
        @pl.loop(1, z)
        def _(k):
            shuf_own_copy(z - k).start()

        send_ends(subj - CORES, start)
        send_rows(0, subj - CORES, start)

    @pl.when(inner)
    def _():
        for load in loads:
            load().start()
        own_shuf.start()

    @pl.when(to_high)
    def _():
        pl.semaphore_wait(up.at[1], 1)
        shuf_own_copy(z + 1).start()
        send_ends(subj + CORES, start)

        @pl.loop(2, last - z)
        def _(d):
            pl.semaphore_wait(up.at[d], 1)
            shuf_own_copy(z + d).start()

        send_rows(1, subj + CORES, start)

    def event(dist, h, act):
        @pl.when(z + dist < n_z)
        def _():
            act(subj + CORES * dist, h, z > 1, subj - CORES)

        @pl.when(z - dist >= 0)
        def _():
            act(subj - CORES * dist, h, z < last - 1, subj + CORES)

    def arrive(slot, h, onward, target):
        pass_copy(slot, h, row_send, sibling).wait_recv()

        @pl.when(onward)
        def _():
            pass_copy(slot, h, row_send, target).start()

        pass_copy(slot, h, sib_send, sibling).start()

    def drain(slot, h, onward, target):
        @pl.when(onward)
        def _():
            pass_copy(slot, h, row_send, target).wait_send()

        pass_copy(slot, h, sib_send, sibling).wait_send()

    def shuf_arrive(subj_slot, h, onward, target):
        slot = perm * n_subj + subj_slot
        shuf_wait(slot)
        for k in range(1, n_plane):
            shuf_in_copy(shuf.at[slot], slot, k).start()

    def shuf_drain(subj_slot, h, onward, target):
        slot = perm * n_subj + subj_slot
        for k in range(1, n_plane):
            shuf_in_copy(shuf.at[slot], slot, k).wait_send()

    in_piece = lax.broadcasted_iota(jnp.int32, (piece, rows), 0)

    def picks_of(p, first, span, l):
        line = shuf[p * n_subj + listed(l)] - first
        bases = [
            g // (PIECES * CORES) * (CORES * rows) + g // CORES % PIECES * piece + g % CORES * rows
            for g in range(span // piece)]
        return jnp.concatenate([(in_piece == line - base).astype(jnp.bfloat16) for base in bases], axis=0)

    span, end_span = SPAN * rows, END_SPAN * rows
    n_ends = gathered.shape[0] // end_span

    def move_own(task):
        p, turn = task // n_spans, lax.rem(task, n_spans)
        picks = [picks_of(p, turn * span, span, l) for l in range(n_list)]
        out = jnp.dot(jnp.concatenate(picks, axis=1), kin_t[...], preferred_element_type=jnp.float32)
        at = pl.ds(pl.multiple_of(turn * span, span), span)
        moved[2 * p, at] = out.astype(jnp.bfloat16)
        moved[2 * p + 1, at] = picks[4]
        moved[2 * (n_perm + p) + 1, at] = picks[0]

    def move_end(p, turn):
        picks = [picks_of(p, turn * end_span, end_span, l) for l in range(SHARED)]
        out = jnp.dot(jnp.concatenate(picks, axis=1), end_t[...], preferred_element_type=jnp.float32)
        at = pl.ds(pl.multiple_of(turn * end_span, end_span), end_span)
        moved[2 * (n_perm + p), at] = out.astype(jnp.bfloat16)

    n_half = n_perm * 2

    def term(q, start, length):
        at = pl.ds(pl.multiple_of(start, rows), length)
        return lax.dot_general(
            moved[q, at], gathered[at], (((0,), (0,)), ((), ())), preferred_element_type=jnp.float32)

    def add(which, start, length, first=False):
        for q in which:
            new = term(q, start, length)
            acc[q] = new if first else acc[q] + new

    def sides(dist, act):
        @pl.loop(0, 2)
        def _(side):
            q = z + dist * (1 - 2 * side)

            @pl.when(jnp.logical_and(q >= 0, q < n_z))
            def _():
                act(q)

    def await_sibling(q, hs):
        for h in hs:
            pass_copy(q * CORES + 1 - core, h, row_send, sibling).wait_recv()

    def turn_block(src, dst, l, scale, clear=False):
        block = jnp.transpose(src[:, l * rows:(l + 1) * rows].astype(jnp.float32)) * scale
        if clear:
            down = lax.broadcasted_iota(jnp.int32, (rows, rows), 0)
            across = lax.broadcasted_iota(jnp.int32, (rows, rows), 1)
            block = jnp.where(down == across, 0.0, block)
        dst[l * rows:(l + 1) * rows] = block.astype(jnp.bfloat16)

    def square_sum(chunk):
        own = gathered[pl.ds(pl.multiple_of(chunk * rows, rows), rows)].astype(jnp.float32)
        return jnp.sum(own * own, axis=0, keepdims=True)


    per_hub = n_subj - 2 * CORES

    def hub_slot(p, s):
        return p * per_hub + s - CORES

    per_z = n_all // n_z

    def fin_copy(k):
        to_z, rest = k // per_z, lax.rem(k, per_z)
        to_perm, to_subj = rest // CORES, to_z * CORES + lax.rem(rest, CORES)
        mine = hub_slot(perm, subj)
        copy = remote(parts.at[to_perm], final.at[mine], fin_send.at[k], fin_recv.at[mine],
                      perm=to_perm, subj=to_subj)
        return copy, to_perm * n_subj + to_subj != me

    @pl.when(inner)
    def _():
        meet(2)
        for h in range(PIECES):
            own_copy(h, 2, sibling).start()
        meet(0)
        launch(across_perm, 0)
        meet(1)
        for load in loads:
            load().wait()
        for l in range(n_list):
            turn_block(kin, kin_t, l, 0.5 if l in (4, 5) else 1.0, clear=l == 4)

        finish_sweep(across_perm, 0)
        launch(across_vert, 1)
        for k in range(1, n_plane):
            shuf_in_copy(shf_hbm, me, k).start()

        def share_end(i):
            @pl.when(by_end)
            def _():
                end_share_copy(i, chip, chip).wait_recv()
                for k in range(1, n_chips):
                    end_share_copy(i, chip, lax.rem(chip + k, n_chips)).start()

        def meet_lines():
            @pl.loop(jnp.where(to_high, last - z, 1), n_z - z)
            def _(d):
                pl.semaphore_wait(up.at[d], 1)

            for k in range(1, n_plane):
                t = lax.rem(perm * CORES + core + k, n_plane)
                signal(lines, perm=t // CORES, subj=z * CORES + lax.rem(t, CORES))

        def await_shuf(p):
            for c in range(CORES):
                @pl.when(p * CORES + c != perm * CORES + core)
                def _():
                    @pl.loop(0, n_z)
                    def _(q):
                        shuf_wait(p * n_subj + q * CORES + c)

        def own_tasks(p, first, end):
            @pl.loop(p * n_spans + first, p * n_spans + end)
            def _(task):
                move_own(task)

        def end_tasks(p):
            @pl.loop(0, n_ends)
            def _(turn):
                move_end(p, turn)

        def take_ends():
            @pl.when(by_end)
            def _():
                @pl.loop(1, n_chips)
                def _(k):
                    for i in range(SHARED):
                        end_share_copy(i, lax.rem(chip + k, n_chips), chip).wait_recv()

                for l in range(SHARED):
                    turn_block(end_kin, end_t, l, 0.5 if l < 2 else 1.0, clear=l == 0)

            @pl.when(jnp.logical_not(by_end))
            def _():
                end_t[...] = jnp.zeros_like(end_t)

        def square_parts():
            parts[0, 1:2] = square_sum(z * 2 + core)

            @pl.when(by_end)
            def _():
                parts[0, 1:2] += square_sum(near * 2 + core)

            for p in range(1, n_perm):
                parts[p, 1:2] = parts[0, 1:2]

        other_hub = last - z

        def hub_piece(h):
            arrive(other_hub * CORES + core, h, z < 0, subj)

        def near_piece(h):
            arrive(near * CORES + core, h, z > 0, other_hub * CORES + core)

        def far_piece(h):
            arrive(far * CORES + core, h, z < 0, subj)

        plane_rows = CORES * rows
        own_m, own_p = [2 * p for p in range(n_perm)], [2 * p + 1 for p in range(n_perm)]
        end_m, end_p = ([n_half + q for q in part] for part in (own_m, own_p))
        short = last == 3

        turns = [lax.rem(perm + k, n_perm) for k in range(n_perm)]
        event(1, 0, shuf_arrive)
        finish_sweep(across_vert, 1)
        share_end(0)

        @pl.loop(2, last)
        def _(dist):
            event(dist, 0, shuf_arrive)

        own_shuf.wait()
        share_end(1)
        share_end(2)
        await_shuf(turns[0])
        if short:
            own_tasks(turns[0], 0, n_spans // 2)
            near_piece(0)
            hub_piece(0)
            hub_piece(1)
            own_tasks(turns[0], n_spans // 2, n_spans)
            near_piece(1)
            hub_piece(2)
            for turn in turns[1:]:
                await_shuf(turn)
                own_tasks(turn, 0, n_spans // 2)
                near_piece(2)
                hub_piece(3)
                own_tasks(turn, n_spans // 2, n_spans)
            near_piece(3)
            meet_lines()
            take_ends()
            for p in range(n_perm):
                end_tasks(p)
                far_piece(p)
            for q in (z, other_hub, near):
                await_sibling(q, range(PIECES))
            square_parts()
            start = (z - 1) * plane_rows
            add(own_m + own_p, start, 3 * plane_rows, first=True)
            far_piece(2)
            add(end_p, start, 3 * plane_rows, first=True)
            far_piece(3)
            add(end_m, start, 3 * plane_rows, first=True)
        else:
            for k, turn in enumerate(turns):
                if k > 0:
                    await_shuf(turn)
                own_tasks(turn, 0, n_spans)

            @pl.loop(1, last)
            def _(dist):
                for h in range(PIECES):
                    event(dist, h, arrive)

            meet_lines()
            await_sibling(z, range(PIECES))
            for dist in range(1, last):
                sides(dist, lambda q: await_sibling(q, range(PIECES)))
            add(own_m + own_p + end_p, plane_rows, (n_z - 2) * plane_rows, first=True)
            take_ends()
            for p in range(n_perm):
                end_tasks(p)
            square_parts()
            add(end_m, plane_rows, (n_z - 2) * plane_rows, first=True)
            add(own_m + own_p + end_p + end_m, near * plane_rows, plane_rows)
        if short:
            await_sibling(far, range(PIECES))
        start = far * plane_rows
        for p in range(n_perm):
            cross = 0.0
            for part in range(2):
                q = part * n_half + 2 * p
                left, right = (acc[i] + term(i, start, plane_rows) for i in (q, q + 1))
                cross += jnp.sum(left * right, axis=0, keepdims=True)
            parts[p, 0:1] = cross

        pl.semaphore_wait(lines, n_plane - 1)

        @pl.loop(0, n_all)
        def _(k):
            copy, other = fin_copy(k)
            pl.when(other)(copy.start)

        final[hub_slot(perm, subj)] = parts[perm]

    @pl.loop(0, n_perm)
    def _(p):
        @pl.loop(CORES, n_subj - CORES)
        def _(s):
            @pl.when(p * n_subj + s != me)
            def _():
                slot = hub_slot(p, s)
                remote(parts.at[0], final.at[slot], fin_send.at[0], fin_recv.at[slot], subj=sibling).wait_recv()

    count = n_subj * rows
    for q in range(n_perm):
        total = jnp.sum(final[q * per_hub:(q + 1) * per_hub], axis=0)
        scale = jnp.sqrt(jnp.float32(count)) * (total[1:2] / count + 1e-05)
        out_ref[:, q * cols:(q + 1) * cols] = 2.0 * total[0:1] / scale

    @pl.when(to_low)
    def _():
        @pl.loop(1, z)
        def _(k):
            shuf_own_copy(z - k).wait_send()

        send_ends(subj - CORES, finish)
        send_rows(0, subj - CORES, finish)

    @pl.when(to_high)
    def _():
        @pl.loop(1, last - z)
        def _(d):
            shuf_own_copy(z + d).wait_send()

        send_ends(subj + CORES, finish)
        send_rows(1, subj + CORES, finish)

    @pl.when(z == 0)
    def _():
        pl.semaphore_wait(up.at[last], 1)

    @pl.when(inner)
    def _():
        for k in range(1, n_plane):
            shuf_in_copy(shf_hbm, me, k).wait_send()
        for h in range(PIECES):
            own_copy(h, 2, sibling).wait_send()

        @pl.loop(1, last)
        def _(dist):
            event(dist, 0, shuf_drain)
            for h in range(PIECES):
                event(dist, h, drain)

        @pl.when(by_end)
        def _():
            for i in range(SHARED):
                for k in range(1, n_chips):
                    end_share_copy(i, chip, lax.rem(chip + k, n_chips)).wait_send()

        @pl.loop(0, n_all)
        def _(k):
            copy, other = fin_copy(k)
            pl.when(other)(copy.wait_send)


def per_device(n_perm, n_subj, n_vert, kinship, phenotype, shuffle):
    rows, width = phenotype.shape
    cols = width // n_perm
    n_all = n_perm * n_subj
    n_z = n_subj // CORES
    n_list = n_z + 3
    n_chips = n_vert * n_perm
    n_hubs = n_perm * (n_subj - 2 * CORES)
    DMA, VMEM = pltpu.SemaphoreType.DMA, pltpu.VMEM
    out = pl.pallas_call(
        functools.partial(kernel, n_perm, n_subj, n_vert),
        out_shape=jax.ShapeDtypeStruct((1, width), jnp.float32),
        in_specs=[pl.BlockSpec(memory_space=pl.ANY)] * 3,
        out_specs=pl.BlockSpec(memory_space=VMEM),
        scratch_shapes=[
            VMEM((rows, n_list * rows), jnp.bfloat16),
            VMEM((rows, SHARED * rows), jnp.bfloat16),
            VMEM((n_list * rows, rows), jnp.bfloat16),
            VMEM((SHARED * rows, rows), jnp.bfloat16),
            VMEM((n_all, 1, rows), jnp.int32),
            VMEM((n_perm * 4, n_subj * rows, rows), jnp.bfloat16),
            VMEM((n_subj * rows, cols), jnp.bfloat16),
            VMEM((n_perm * 4, rows, cols), jnp.float32),
            VMEM((n_perm, 2, cols), jnp.float32),
            VMEM((n_hubs, 2, cols), jnp.float32),
            DMA((PIECES + n_list + 1,)),
            pltpu.SemaphoreType.REGULAR((n_z,)), pltpu.SemaphoreType.REGULAR((3,)),
            pltpu.SemaphoreType.REGULAR((2,)), pltpu.SemaphoreType.REGULAR((2,)), pltpu.SemaphoreType.REGULAR,
            DMA((n_all,)), DMA((n_z,)), DMA((n_subj, n_perm * CORES)),
            DMA((n_subj, PIECES)), DMA((3, PIECES)), DMA((n_subj, PIECES)), DMA((n_subj, PIECES)),
            DMA((n_chips, SHARED)), DMA((SHARED,)), DMA((SHARED, n_chips)),
            DMA((n_all,)), DMA((n_hubs,)),
        ],
        compiler_params=pltpu.CompilerParams(collective_id=0, has_side_effects=True),
    )(kinship, phenotype, shuffle.reshape(1, rows))
    return out.reshape(width)


def solution(mesh):
    in_specs = (P("subj", None), P("subj", "vert"), P(("perm", "subj")))
    out_specs = P(("perm", "vert"))
    sizes = [mesh.shape[axis] for axis in ("perm", "subj", "vert")]
    body = functools.partial(per_device, *sizes)
    return jax.shard_map(body, mesh=mesh, in_specs=in_specs, out_specs=out_specs, check_vma=False)
```

```python
import functools

import jax
import jax.numpy as jnp
from jax import lax
from jax.experimental import pallas as pl
from jax.experimental.pallas import tpu as pltpu
from jax.sharding import PartitionSpec as P

MESH = pl.DeviceIdType.MESH
CORES = 2
PIECES = 4
SHARED = 3
SPAN = 4
END_SPAN = 4


def kernel(
    n_perm, n_subj, n_vert,
    kin_hbm, phe_hbm, shf_hbm, out_ref,
    kin, end_kin, kin_t, end_t, shuf, moved, gathered, acc, parts, final, sent,
    load_sem, up, side, across_perm, across_vert, lines,
    line_recv, group_recv, shuf_own, shuf_in,
    row_recv, sib_recv, own_send, row_send, sib_send,
    end_recv, peer_recv, end_send, end_share, fin_send, fin_recv,
):
    perm, subj, vert = lax.axis_index("perm"), lax.axis_index("subj"), lax.axis_index("vert")
    n_all = n_perm * n_subj
    me = perm * n_subj + subj
    z, core = subj // CORES, lax.rem(subj, CORES)
    n_z = n_subj // CORES
    last = n_z - 1
    sibling = z * CORES + (1 - core)
    rows, cols = kin.shape[0], gathered.shape[1]
    piece = rows // PIECES
    n_list = kin.shape[1] // rows
    n_spans = gathered.shape[0] // (SPAN * rows)
    n_plane = n_perm * CORES
    n_chips = n_vert * n_perm
    chip = vert * n_perm + perm
    share = rows // n_chips
    inner = jnp.logical_and(z > 0, z < last)
    by_end = jnp.logical_or(z == 1, z == last - 1)
    first_col = pl.multiple_of(perm * cols, cols)
    barrier = pltpu.get_barrier_semaphore()

    def signal(sem, **device):
        pl.semaphore_signal(sem, inc=1, device_id=device, device_id_type=MESH)

    def half(h):
        return pl.ds(pl.multiple_of(h * piece, piece), piece)

    def spot(q, c, h):
        at = pl.multiple_of((q * PIECES + h) * (CORES * piece) + c * piece, piece)
        return gathered.at[pl.ds(at, piece)]

    near = jnp.where(z * 2 < n_z, 0, last)
    far = last - near
    low_end = near == 0
    far_core = jnp.where(low_end, core, 1 - core)

    def listed(l):
        if l == 0:
            return near * CORES + core
        if l == 1:
            return near * CORES + 1 - core
        if l == 2:
            return far * CORES + far_core
        if l == 3:
            return far * CORES + 1 - far_core
        if l == 4:
            return subj
        if l == 5:
            return sibling
        k = l - 5
        other = jnp.where(k < z, k, k + 1)
        return other * CORES + jnp.where(other > z, core, 1 - core)

    def kin_load(l):
        block = pl.multiple_of(listed(l) * rows, rows)
        return pltpu.make_async_copy(
            kin_hbm.at[:, pl.ds(block, rows)], kin.at[:, l * rows:(l + 1) * rows], load_sem.at[0])

    def phe_load(h):
        return pltpu.make_async_copy(
            phe_hbm.at[half(h), pl.ds(first_col, cols)], spot(z, core, h), load_sem.at[1])

    own_shuf = pltpu.make_async_copy(shf_hbm, shuf.at[me], load_sem.at[2])
    loads = [functools.partial(kin_load, l) for l in range(n_list)]
    loads += [functools.partial(phe_load, h) for h in range(PIECES)]

    @pl.loop(z + 1, n_z)
    def _(q):
        signal(barrier, subj=q * CORES + core)

    axes = (
        (perm, n_perm, lambda d: dict(perm=perm + d)),
        (vert, n_vert, lambda d: dict(vert=vert + d)),
        (core, CORES, lambda d: dict(subj=subj + d)),
    )
    for index, size, near_by in axes:
        @pl.when(jnp.logical_and(inner, index < size - 1))
        def _():
            signal(barrier, **near_by(1))

    lower = sum((index > 0).astype(jnp.int32) for index, _, _ in axes)
    lower = z + jnp.where(inner, lower, 0)

    @pl.when(lower > 0)
    def _():
        pl.semaphore_wait(barrier, lower)

    @pl.loop(1, z + 1)
    def _(d):
        signal(up.at[d], subj=subj - CORES * d)

    def answer_plane():
        for i, (index, size, near_by) in enumerate(axes):
            @pl.when(index > 0)
            def _():
                signal(side.at[i], **near_by(-1))

    def meet(i):
        index, size, _ = axes[i]

        @pl.when(index < size - 1)
        def _():
            pl.semaphore_wait(side.at[i], 1)

    def sweep_ways(sem, i):
        index, size, near_by = axes[i]
        up_side, down_side = index < size - 1, index > 0
        return (
            (sem.at[0], lambda done: signal(done, **near_by(1)), down_side, up_side),
            (sem.at[1], lambda done: signal(done, **near_by(-1)), up_side, down_side),
        )

    def launch(sem, i):
        for done, tell, behind, ahead in sweep_ways(sem, i):
            pl.when(jnp.logical_and(ahead, jnp.logical_not(behind)))(functools.partial(tell, done))

    def finish_sweep(sem, i):
        for done, tell, behind, ahead in sweep_ways(sem, i):
            @pl.when(behind)
            def _():
                pl.semaphore_wait(done, 1)
                pl.when(ahead)(functools.partial(tell, done))

    def remote(src, dst, send, recv, **device):
        return pltpu.make_async_remote_copy(
            src_ref=src, dst_ref=dst, send_sem=send, recv_sem=recv, device_id=device, device_id_type=MESH)

    def await_sent(ref, sem):
        remote(ref, ref, sem, sem, subj=sibling).wait_send()

    def await_all(ref, sem):
        remote(ref, ref, sem, sem, subj=sibling).wait_recv()

    def own_copy(h, way, target):
        return remote(
            phe_hbm.at[half(h), pl.ds(first_col, cols)], spot(z, core, h),
            own_send.at[way], row_recv.at[z, h], subj=target)

    def own_sib_copy(h):
        return remote(
            phe_hbm.at[half(h), pl.ds(first_col, cols)], spot(z, core, h), sib_send, sib_recv.at[z], subj=sibling)

    def pass_copy(q, h, target):
        here = spot(q, core, h)
        return remote(here, here, row_send.at[q], row_recv.at[q, h], subj=target)

    def sib_copy(q, h):
        here = spot(q, core, h)
        return remote(here, here, sib_send, sib_recv.at[q], subj=sibling)

    def shuf_own_copy(q):
        return remote(shf_hbm, shuf.at[me], shuf_own, line_recv.at[z], subj=q * CORES + core)

    def shuf_in_copy(src, q, k):
        t = lax.rem(perm * CORES + core + k, n_plane)
        slot = perm * n_subj + q * CORES + core
        return remote(src, shuf.at[slot], shuf_in, group_recv.at[perm * CORES + core],
                      perm=t // CORES, subj=z * CORES + lax.rem(t, CORES))

    def part_of(owner):
        return pl.ds(pl.multiple_of(owner * share, share), share)

    def end_block(i):
        end_core = core if i == 0 else 1 - core
        if i < 2:
            return z * CORES + end_core
        return jnp.where(z == 0, last * CORES + core, 1 - core)

    def end_copy(i, target):
        block = pl.multiple_of(end_block(i) * rows, rows)
        return remote(
            kin_hbm.at[part_of(chip), pl.ds(block, rows)], end_kin.at[part_of(chip), i * rows:(i + 1) * rows],
            end_send, end_recv.at[i], subj=target)

    def end_share_copy(i, owner, t):
        here = end_kin.at[part_of(owner), i * rows:(i + 1) * rows]
        return remote(here, here, end_share, peer_recv, vert=t // n_perm, perm=lax.rem(t, n_perm))

    def send_ends(target):
        @pl.when(jnp.logical_not(inner))
        def _():
            for i in range(SHARED):
                end_copy(i, target).start()

    def send_rows(way, target):
        for h in range(PIECES):
            own_copy(h, way, target).start()

    to_low, to_high = z >= 2, z <= last - 2

    pl.when(inner)(answer_plane)

    @pl.when(to_low)
    def _():
        @pl.loop(1, z)
        def _(k):
            shuf_own_copy(z - k).start()

        send_ends(subj - CORES)
        send_rows(0, subj - CORES)

    @pl.when(inner)
    def _():
        for load in loads:
            load().start()
        own_shuf.start()

    @pl.when(to_high)
    def _():
        pl.semaphore_wait(up.at[1], 1)
        shuf_own_copy(z + 1).start()
        send_ends(subj + CORES)

        @pl.loop(2, last - z)
        def _(d):
            pl.semaphore_wait(up.at[d], 1)
            shuf_own_copy(z + d).start()

        send_rows(1, subj + CORES)

    def event(dist, h, act):
        @pl.when(z + dist < n_z)
        def _():
            act(z + dist, h, z > 1, subj - CORES)

        @pl.when(z - dist >= 0)
        def _():
            act(z - dist, h, z < last - 1, subj + CORES)

    def arrive(q, h, onward, target):
        pass_copy(q, h, sibling).wait_recv()

        @pl.when(onward)
        def _():
            pass_copy(q, h, target).start()

        sib_copy(q, h).start()

    def drain(q, h, onward, target):
        @pl.when(onward)
        def _():
            await_sent(gathered.at[0:rows], row_send.at[q])

    def shuf_arrive(q, h, onward, target):
        slot = perm * n_subj + q * CORES + core
        await_all(shuf.at[slot], line_recv.at[q])
        for k in range(1, n_plane):
            shuf_in_copy(shuf.at[slot], q, k).start()

    in_piece = lax.broadcasted_iota(jnp.int32, (piece, rows), 0)

    def picks_of(p, first, span, l):
        line = shuf[p * n_subj + listed(l)] - first
        bases = [
            g // (PIECES * CORES) * (CORES * rows) + g // CORES % PIECES * piece + g % CORES * rows
            for g in range(span // piece)]
        return jnp.concatenate([(in_piece == line - base).astype(jnp.bfloat16) for base in bases], axis=0)

    span, end_span = SPAN * rows, END_SPAN * rows
    n_ends = gathered.shape[0] // end_span

    def move_own(task):
        p, turn = task // n_spans, lax.rem(task, n_spans)
        picks = [picks_of(p, turn * span, span, l) for l in range(n_list)]
        out = jnp.dot(jnp.concatenate(picks, axis=1), kin_t[...], preferred_element_type=jnp.float32)
        at = pl.ds(pl.multiple_of(turn * span, span), span)
        moved[2 * p, at] = out.astype(jnp.bfloat16)
        moved[2 * p + 1, at] = picks[4]
        moved[2 * (n_perm + p) + 1, at] = picks[0]

    def move_end(p, turn):
        picks = [picks_of(p, turn * end_span, end_span, l) for l in range(SHARED)]
        out = jnp.dot(jnp.concatenate(picks, axis=1), end_t[...], preferred_element_type=jnp.float32)
        at = pl.ds(pl.multiple_of(turn * end_span, end_span), end_span)
        moved[2 * (n_perm + p), at] = out.astype(jnp.bfloat16)

    n_half = n_perm * 2

    def term(q, start, length):
        at = pl.ds(pl.multiple_of(start, rows), length)
        return lax.dot_general(
            moved[q, at], gathered[at], (((0,), (0,)), ((), ())), preferred_element_type=jnp.float32)

    def add(which, start, length, first=False):
        for q in which:
            new = term(q, start, length)
            acc[q] = new if first else acc[q] + new

    def sides(dist, act):
        @pl.loop(0, 2)
        def _(side):
            q = z + dist * (1 - 2 * side)

            @pl.when(jnp.logical_and(q >= 0, q < n_z))
            def _():
                act(q)

    def await_sibling(q):
        await_all(gathered.at[0:rows], sib_recv.at[q])

    def turn_block(src, dst, l, scale, clear=False):
        block = jnp.transpose(src[:, l * rows:(l + 1) * rows].astype(jnp.float32)) * scale
        if clear:
            down = lax.broadcasted_iota(jnp.int32, (rows, rows), 0)
            across = lax.broadcasted_iota(jnp.int32, (rows, rows), 1)
            block = jnp.where(down == across, 0.0, block)
        dst[l * rows:(l + 1) * rows] = block.astype(jnp.bfloat16)

    def square_sum(chunk):
        own = gathered[pl.ds(pl.multiple_of(chunk * rows, rows), rows)].astype(jnp.float32)
        return jnp.sum(own * own, axis=0, keepdims=True)


    per_hub = n_subj - 2 * CORES

    def hub_slot(p, s):
        return p * per_hub + s - CORES

    per_z = n_all // n_z

    def fin_copy(k):
        to_z, rest = k // per_z, lax.rem(k, per_z)
        to_perm, to_subj = rest // CORES, to_z * CORES + lax.rem(rest, CORES)
        mine = hub_slot(perm, subj)
        copy = remote(parts.at[to_perm], final.at[mine], fin_send, fin_recv,
                      perm=to_perm, subj=to_subj)
        return copy, to_perm * n_subj + to_subj != me

    @pl.when(inner)
    def _():
        meet(2)
        for h in range(PIECES):
            own_sib_copy(h).start()
        meet(0)
        launch(across_perm, 0)
        meet(1)
        pltpu.make_async_copy(kin, kin, load_sem.at[0]).wait()
        pltpu.make_async_copy(gathered.at[0:rows], gathered.at[0:rows], load_sem.at[1]).wait()
        for l in range(n_list):
            turn_block(kin, kin_t, l, 0.5 if l in (4, 5) else 1.0, clear=l == 4)

        finish_sweep(across_perm, 0)
        launch(across_vert, 1)
        for k in range(1, n_plane):
            shuf_in_copy(shf_hbm, z, k).start()

        def share_end(i):
            @pl.when(by_end)
            def _():
                end_copy(i, sibling).wait_recv()
                for k in range(1, n_chips):
                    end_share_copy(i, chip, lax.rem(chip + k, n_chips)).start()

        def meet_lines():
            @pl.loop(jnp.where(to_high, last - z, 1), n_z - z)
            def _(d):
                pl.semaphore_wait(up.at[d], 1)

            for k in range(1, n_plane):
                t = lax.rem(perm * CORES + core + k, n_plane)
                signal(lines, perm=t // CORES, subj=z * CORES + lax.rem(t, CORES))

        def await_shuf(p):
            for c in range(CORES):
                @pl.when(p * CORES + c != perm * CORES + core)
                def _():
                    await_all(shuf.at[0:n_z], group_recv.at[p * CORES + c])

        def own_tasks(p, first, end):
            @pl.loop(p * n_spans + first, p * n_spans + end)
            def _(task):
                move_own(task)

        def end_tasks(p):
            @pl.loop(0, n_ends)
            def _(turn):
                move_end(p, turn)

        def take_ends():
            @pl.when(by_end)
            def _():
                await_all(end_kin.at[0:(n_chips - 1) * share], peer_recv)
                for l in range(SHARED):
                    turn_block(end_kin, end_t, l, 0.5 if l < 2 else 1.0, clear=l == 0)

            @pl.when(jnp.logical_not(by_end))
            def _():
                end_t[...] = jnp.zeros_like(end_t)

        def square_parts():
            parts[0, 1:2] = square_sum(z * 2 + core)

            @pl.when(by_end)
            def _():
                parts[0, 1:2] += square_sum(near * 2 + core)

            for p in range(1, n_perm):
                parts[p, 1:2] = parts[0, 1:2]

        other_hub = last - z

        def hub_piece(h):
            arrive(other_hub, h, z < 0, subj)

        def near_piece(h):
            arrive(near, h, z > 0, other_hub * CORES + core)

        def far_piece(h):
            arrive(far, h, z < 0, subj)

        plane_rows = CORES * rows
        own_m, own_p = [2 * p for p in range(n_perm)], [2 * p + 1 for p in range(n_perm)]
        end_m, end_p = ([n_half + q for q in part] for part in (own_m, own_p))
        short = last == 3

        turns = [lax.rem(perm + k, n_perm) for k in range(n_perm)]
        event(1, 0, shuf_arrive)
        finish_sweep(across_vert, 1)
        share_end(0)

        @pl.loop(2, last)
        def _(dist):
            event(dist, 0, shuf_arrive)

        own_shuf.wait()
        share_end(1)
        share_end(2)
        await_shuf(turns[0])
        if short:
            own_tasks(turns[0], 0, n_spans // 2)
            near_piece(0)
            hub_piece(0)
            hub_piece(1)
            own_tasks(turns[0], n_spans // 2, n_spans)
            near_piece(1)
            hub_piece(2)
            for turn in turns[1:]:
                await_shuf(turn)
                own_tasks(turn, 0, n_spans // 2)
                near_piece(2)
                hub_piece(3)
                own_tasks(turn, n_spans // 2, n_spans)
            near_piece(3)
            meet_lines()
            take_ends()
            for p in range(n_perm):
                end_tasks(p)
                far_piece(p)
            for q in (z, other_hub, near):
                await_sibling(q)
            square_parts()
            start = (z - 1) * plane_rows
            add(own_m + own_p, start, 3 * plane_rows, first=True)
            far_piece(2)
            add(end_p, start, 3 * plane_rows, first=True)
            far_piece(3)
            add(end_m, start, 3 * plane_rows, first=True)
        else:
            for k, turn in enumerate(turns):
                if k > 0:
                    await_shuf(turn)
                own_tasks(turn, 0, n_spans)

            @pl.loop(1, last)
            def _(dist):
                for h in range(PIECES):
                    event(dist, h, arrive)

            meet_lines()
            await_sibling(z)
            for dist in range(1, last):
                sides(dist, lambda q: await_sibling(q))
            add(own_m + own_p + end_p, plane_rows, (n_z - 2) * plane_rows, first=True)
            take_ends()
            for p in range(n_perm):
                end_tasks(p)
            square_parts()
            add(end_m, plane_rows, (n_z - 2) * plane_rows, first=True)
            add(own_m + own_p + end_p + end_m, near * plane_rows, plane_rows)
        if short:
            await_sibling(far)
        start = far * plane_rows
        for p in range(n_perm):
            cross = 0.0
            for part in range(2):
                q = part * n_half + 2 * p
                left, right = (acc[i] + term(i, start, plane_rows) for i in (q, q + 1))
                cross += jnp.sum(left * right, axis=0, keepdims=True)
            parts[p, 0:1] = cross

        pl.semaphore_wait(lines, n_plane - 1)

        @pl.loop(0, n_all)
        def _(k):
            copy, other = fin_copy(k)
            pl.when(other)(copy.start)

        final[hub_slot(perm, subj)] = parts[perm]

    n_hubs = n_perm * per_hub

    @pl.when(inner)
    def _():
        await_all(final.at[0:n_hubs - 1], fin_recv)

    @pl.when(jnp.logical_not(inner))
    def _():
        await_all(final, fin_recv)

    count = n_subj * rows
    for q in range(n_perm):
        total = jnp.sum(final[q * per_hub:(q + 1) * per_hub], axis=0)
        scale = jnp.sqrt(jnp.float32(count)) * (total[1:2] / count + 1e-05)
        out_ref[:, q * cols:(q + 1) * cols] = 2.0 * total[0:1] / scale

    for way, sending in enumerate((to_low, to_high)):
        @pl.when(sending)
        def _():
            await_sent(gathered.at[0:rows], own_send.at[way])

    @pl.when(inner)
    def _():
        await_sent(shuf.at[0:n_z - 3], shuf_own)
        await_sent(shuf.at[0:n_z * (n_plane - 1)], shuf_in)
        await_sent(gathered.at[0:n_z * rows], sib_send)

        @pl.loop(1, last)
        def _(dist):
            event(dist, 0, drain)

        @pl.when(by_end)
        def _():
            await_sent(end_kin.at[0:(n_chips - 1) * share], end_share)

        await_sent(sent, fin_send)

    @pl.when(jnp.logical_not(inner))
    def _():
        await_sent(shuf.at[0:n_z - 2], shuf_own)
        await_sent(end_kin.at[0:share], end_send)

    @pl.when(z == 0)
    def _():
        pl.semaphore_wait(up.at[last], 1)


def per_device(n_perm, n_subj, n_vert, kinship, phenotype, shuffle):
    rows, width = phenotype.shape
    cols = width // n_perm
    n_all = n_perm * n_subj
    n_z = n_subj // CORES
    n_list = n_z + 3
    n_chips = n_vert * n_perm
    n_hubs = n_perm * (n_subj - 2 * CORES)
    DMA, VMEM = pltpu.SemaphoreType.DMA, pltpu.VMEM
    out = pl.pallas_call(
        functools.partial(kernel, n_perm, n_subj, n_vert),
        out_shape=jax.ShapeDtypeStruct((1, width), jnp.float32),
        in_specs=[pl.BlockSpec(memory_space=pl.ANY)] * 3,
        out_specs=pl.BlockSpec(memory_space=VMEM),
        scratch_shapes=[
            VMEM((rows, n_list * rows), jnp.bfloat16),
            VMEM((rows, SHARED * rows), jnp.bfloat16),
            VMEM((n_list * rows, rows), jnp.bfloat16),
            VMEM((SHARED * rows, rows), jnp.bfloat16),
            VMEM((n_all, 1, rows), jnp.int32),
            VMEM((n_perm * 4, n_subj * rows, rows), jnp.bfloat16),
            VMEM((n_subj * rows, cols), jnp.bfloat16),
            VMEM((n_perm * 4, rows, cols), jnp.float32),
            VMEM((n_perm, 2, cols), jnp.float32),
            VMEM((n_hubs, 2, cols), jnp.float32),
            VMEM((n_all - 1, 2, cols), jnp.float32),
            DMA((3,)),
            pltpu.SemaphoreType.REGULAR((n_z,)), pltpu.SemaphoreType.REGULAR((3,)),
            pltpu.SemaphoreType.REGULAR((2,)), pltpu.SemaphoreType.REGULAR((2,)), pltpu.SemaphoreType.REGULAR,
            DMA((n_z,)), DMA((n_perm * CORES,)), DMA, DMA,
            DMA((n_z, PIECES)), DMA((n_z,)), DMA((2,)), DMA((n_z,)), DMA,
            DMA((SHARED,)), DMA, DMA, DMA, DMA, DMA,
        ],
        compiler_params=pltpu.CompilerParams(collective_id=0, has_side_effects=True),
    )(kinship, phenotype, shuffle.reshape(1, rows))
    return out.reshape(width)


def solution(mesh):
    in_specs = (P("subj", None), P("subj", "vert"), P(("perm", "subj")))
    out_specs = P(("perm", "vert"))
    sizes = [mesh.shape[axis] for axis in ("perm", "subj", "vert")]
    body = functools.partial(per_device, *sizes)
    return jax.shard_map(body, mesh=mesh, in_specs=in_specs, out_specs=out_specs, check_vma=False)
```

```python
import functools

import jax
import jax.numpy as jnp
from jax import lax
from jax.experimental import pallas as pl
from jax.experimental.pallas import tpu as pltpu
from jax.sharding import PartitionSpec as P

MESH = pl.DeviceIdType.MESH
CORES = 2
PIECES = 4
SHARED = 3
SPAN = 4
END_SPAN = 4


def kernel(
    n_perm, n_subj, n_vert,
    kin_hbm, phe_hbm, shf_hbm, out_ref,
    kin, end_kin, kin_t, end_t, shuf, moved, gathered, acc, parts, final, sent,
    load_sem, up, side, across_perm, across_vert, lines,
    line_recv, group_recv, shuf_own, shuf_in,
    row_recv, sib_recv, own_send, row_send, sib_send,
    end_recv, peer_recv, end_send, end_share, fin_send, fin_recv,
):
    perm, subj, vert = lax.axis_index("perm"), lax.axis_index("subj"), lax.axis_index("vert")
    n_all = n_perm * n_subj
    me = perm * n_subj + subj
    z, core = subj // CORES, lax.rem(subj, CORES)
    n_z = n_subj // CORES
    last = n_z - 1
    sibling = z * CORES + (1 - core)
    rows, cols = kin.shape[0], gathered.shape[1]
    piece = rows // PIECES
    n_list = kin.shape[1] // rows
    n_spans = gathered.shape[0] // (SPAN * rows)
    n_plane = n_perm * CORES
    n_chips = n_vert * n_perm
    chip = vert * n_perm + perm
    share = rows // n_chips
    inner = jnp.logical_and(z > 0, z < last)
    by_end = jnp.logical_or(z == 1, z == last - 1)
    first_col = pl.multiple_of(perm * cols, cols)
    barrier = pltpu.get_barrier_semaphore()

    def signal(sem, **device):
        pl.semaphore_signal(sem, inc=1, device_id=device, device_id_type=MESH)

    def half(h):
        return pl.ds(pl.multiple_of(h * piece, piece), piece)

    def spot(q, c, h):
        at = pl.multiple_of((q * CORES + c) * rows + h * piece, piece)
        return gathered.at[pl.ds(at, piece)]

    near = jnp.where(z * 2 < n_z, 0, last)
    far = last - near
    low_end = near == 0
    far_core = jnp.where(low_end, core, 1 - core)

    def listed(l):
        if l == 0:
            return near * CORES + core
        if l == 1:
            return near * CORES + 1 - core
        if l == 2:
            return far * CORES + far_core
        if l == 3:
            return far * CORES + 1 - far_core
        if l == 4:
            return subj
        if l == 5:
            return sibling
        k = l - 5
        other = jnp.where(k < z, k, k + 1)
        return other * CORES + jnp.where(other > z, core, 1 - core)

    def kin_load(l):
        block = pl.multiple_of(listed(l) * rows, rows)
        return pltpu.make_async_copy(
            kin_hbm.at[:, pl.ds(block, rows)], kin.at[:, l * rows:(l + 1) * rows], load_sem.at[0])

    def phe_load(h):
        return pltpu.make_async_copy(
            phe_hbm.at[half(h), pl.ds(first_col, cols)], spot(z, core, h), load_sem.at[1])

    own_shuf = pltpu.make_async_copy(shf_hbm, shuf.at[me], load_sem.at[2])
    loads = [functools.partial(kin_load, l) for l in range(n_list)]
    loads += [functools.partial(phe_load, h) for h in range(PIECES)]

    @pl.loop(z + 1, n_z)
    def _(q):
        signal(barrier, subj=q * CORES + core)

    axes = (
        (perm, n_perm, lambda d: dict(perm=perm + d)),
        (vert, n_vert, lambda d: dict(vert=vert + d)),
        (core, CORES, lambda d: dict(subj=subj + d)),
    )
    for index, size, near_by in axes:
        @pl.when(jnp.logical_and(inner, index < size - 1))
        def _():
            signal(barrier, **near_by(1))

    lower = sum((index > 0).astype(jnp.int32) for index, _, _ in axes)
    lower = z + jnp.where(inner, lower, 0)

    @pl.when(lower > 0)
    def _():
        pl.semaphore_wait(barrier, lower)

    @pl.loop(1, z + 1)
    def _(d):
        signal(up.at[d], subj=subj - CORES * d)

    def answer_plane():
        for i, (index, size, near_by) in enumerate(axes):
            @pl.when(index > 0)
            def _():
                signal(side.at[i], **near_by(-1))

    def meet(i):
        index, size, _ = axes[i]

        @pl.when(index < size - 1)
        def _():
            pl.semaphore_wait(side.at[i], 1)

    def sweep_ways(sem, i):
        index, size, near_by = axes[i]
        up_side, down_side = index < size - 1, index > 0
        return (
            (sem.at[0], lambda done: signal(done, **near_by(1)), down_side, up_side),
            (sem.at[1], lambda done: signal(done, **near_by(-1)), up_side, down_side),
        )

    def launch(sem, i):
        for done, tell, behind, ahead in sweep_ways(sem, i):
            pl.when(jnp.logical_and(ahead, jnp.logical_not(behind)))(functools.partial(tell, done))

    def finish_sweep(sem, i):
        for done, tell, behind, ahead in sweep_ways(sem, i):
            @pl.when(behind)
            def _():
                pl.semaphore_wait(done, 1)
                pl.when(ahead)(functools.partial(tell, done))

    def remote(src, dst, send, recv, **device):
        return pltpu.make_async_remote_copy(
            src_ref=src, dst_ref=dst, send_sem=send, recv_sem=recv, device_id=device, device_id_type=MESH)

    def await_sent(ref, sem):
        remote(ref, ref, sem, sem, subj=sibling).wait_send()

    def await_all(ref, sem):
        remote(ref, ref, sem, sem, subj=sibling).wait_recv()

    def own_copy(h, way, target):
        return remote(
            phe_hbm.at[half(h), pl.ds(first_col, cols)], spot(z, core, h),
            own_send.at[way], row_recv.at[z, h], subj=target)

    def own_sib_copy(h):
        return remote(
            phe_hbm.at[half(h), pl.ds(first_col, cols)], spot(z, core, h), sib_send, sib_recv.at[z], subj=sibling)

    def pass_copy(q, h, target):
        here = spot(q, core, h)
        return remote(here, here, row_send.at[q], row_recv.at[q, h], subj=target)

    def sib_copy(q, h):
        here = spot(q, core, h)
        return remote(here, here, sib_send, sib_recv.at[q], subj=sibling)

    def shuf_own_copy(q):
        return remote(shf_hbm, shuf.at[me], shuf_own, line_recv.at[z], subj=q * CORES + core)

    def shuf_in_copy(src, q, k):
        t = lax.rem(perm * CORES + core + k, n_plane)
        slot = perm * n_subj + q * CORES + core
        return remote(src, shuf.at[slot], shuf_in, group_recv.at[perm * CORES + core],
                      perm=t // CORES, subj=z * CORES + lax.rem(t, CORES))

    def part_of(owner):
        return pl.ds(pl.multiple_of(owner * share, share), share)

    def end_block(i):
        end_core = core if i == 0 else 1 - core
        if i < 2:
            return z * CORES + end_core
        return jnp.where(z == 0, last * CORES + core, 1 - core)

    def end_copy(i, target):
        block = pl.multiple_of(end_block(i) * rows, rows)
        return remote(
            kin_hbm.at[part_of(chip), pl.ds(block, rows)], end_kin.at[part_of(chip), i * rows:(i + 1) * rows],
            end_send, end_recv.at[i], subj=target)

    def end_share_copy(i, owner, t):
        here = end_kin.at[part_of(owner), i * rows:(i + 1) * rows]
        return remote(here, here, end_share, peer_recv, vert=t // n_perm, perm=lax.rem(t, n_perm))

    def send_ends(target):
        @pl.when(jnp.logical_not(inner))
        def _():
            for i in range(SHARED):
                end_copy(i, target).start()

    def send_rows(way, target):
        for h in range(PIECES):
            own_copy(h, way, target).start()

    to_low, to_high = z >= 2, z <= last - 2

    pl.when(inner)(answer_plane)

    @pl.when(to_low)
    def _():
        @pl.loop(1, z)
        def _(k):
            shuf_own_copy(z - k).start()

        send_ends(subj - CORES)
        send_rows(0, subj - CORES)

    @pl.when(inner)
    def _():
        for load in loads:
            load().start()
        own_shuf.start()

    @pl.when(to_high)
    def _():
        pl.semaphore_wait(up.at[1], 1)
        shuf_own_copy(z + 1).start()
        send_ends(subj + CORES)

        @pl.loop(2, last - z)
        def _(d):
            pl.semaphore_wait(up.at[d], 1)
            shuf_own_copy(z + d).start()

        send_rows(1, subj + CORES)

    def event(dist, h, act):
        @pl.when(z + dist < n_z)
        def _():
            act(z + dist, h, z > 1, subj - CORES)

        @pl.when(z - dist >= 0)
        def _():
            act(z - dist, h, z < last - 1, subj + CORES)

    def arrive(q, h, onward, target):
        pass_copy(q, h, sibling).wait_recv()

        @pl.when(onward)
        def _():
            pass_copy(q, h, target).start()

        sib_copy(q, h).start()

    def drain(q, h, onward, target):
        @pl.when(onward)
        def _():
            await_sent(gathered.at[0:rows], row_send.at[q])

    def shuf_arrive(q, h, onward, target):
        slot = perm * n_subj + q * CORES + core
        await_all(shuf.at[slot], line_recv.at[q])
        for k in range(1, n_plane):
            shuf_in_copy(shuf.at[slot], q, k).start()

    def picks_of(p, first, span, l):
        subject = lax.broadcasted_iota(jnp.int32, (span, rows), 0) + first
        return (subject == shuf[p * n_subj + listed(l)]).astype(jnp.bfloat16)

    span, end_span = SPAN * rows, END_SPAN * rows
    n_ends = gathered.shape[0] // end_span

    def move_own(task):
        p, turn = task // n_spans, lax.rem(task, n_spans)
        picks = [picks_of(p, turn * span, span, l) for l in range(n_list)]
        out = jnp.dot(jnp.concatenate(picks, axis=1), kin_t[...], preferred_element_type=jnp.float32)
        at = pl.ds(pl.multiple_of(turn * span, span), span)
        moved[2 * p, at] = out.astype(jnp.bfloat16)
        moved[2 * p + 1, at] = picks[4]
        moved[2 * (n_perm + p) + 1, at] = picks[0]

    def move_end(p, turn):
        picks = [picks_of(p, turn * end_span, end_span, l) for l in range(SHARED)]
        out = jnp.dot(jnp.concatenate(picks, axis=1), end_t[...], preferred_element_type=jnp.float32)
        at = pl.ds(pl.multiple_of(turn * end_span, end_span), end_span)
        moved[2 * (n_perm + p), at] = out.astype(jnp.bfloat16)

    n_half = n_perm * 2

    def term(q, start, length):
        at = pl.ds(pl.multiple_of(start, rows), length)
        return lax.dot_general(
            moved[q, at], gathered[at], (((0,), (0,)), ((), ())), preferred_element_type=jnp.float32)

    def add(which, start, length, first=False):
        for q in which:
            new = term(q, start, length)
            acc[q] = new if first else acc[q] + new

    def sides(dist, act):
        @pl.loop(0, 2)
        def _(side):
            q = z + dist * (1 - 2 * side)

            @pl.when(jnp.logical_and(q >= 0, q < n_z))
            def _():
                act(q)

    def await_sibling(q):
        await_all(gathered.at[0:rows], sib_recv.at[q])

    def turn_block(src, dst, l, scale, clear=False):
        block = jnp.transpose(src[:, l * rows:(l + 1) * rows].astype(jnp.float32)) * scale
        if clear:
            down = lax.broadcasted_iota(jnp.int32, (rows, rows), 0)
            across = lax.broadcasted_iota(jnp.int32, (rows, rows), 1)
            block = jnp.where(down == across, 0.0, block)
        dst[l * rows:(l + 1) * rows] = block.astype(jnp.bfloat16)

    def square_sum(chunk):
        own = gathered[pl.ds(pl.multiple_of(chunk * rows, rows), rows)].astype(jnp.float32)
        return jnp.sum(own * own, axis=0, keepdims=True)


    per_hub = n_subj - 2 * CORES

    def hub_slot(p, s):
        return p * per_hub + s - CORES

    per_z = n_all // n_z

    def fin_copy(k):
        to_z, rest = k // per_z, lax.rem(k, per_z)
        to_perm, to_subj = rest // CORES, to_z * CORES + lax.rem(rest, CORES)
        mine = hub_slot(perm, subj)
        copy = remote(parts.at[to_perm], final.at[mine], fin_send, fin_recv,
                      perm=to_perm, subj=to_subj)
        return copy, to_perm * n_subj + to_subj != me

    @pl.when(inner)
    def _():
        meet(2)
        for h in range(PIECES):
            own_sib_copy(h).start()
        meet(0)
        launch(across_perm, 0)
        meet(1)
        pltpu.make_async_copy(kin, kin, load_sem.at[0]).wait()
        pltpu.make_async_copy(gathered.at[0:rows], gathered.at[0:rows], load_sem.at[1]).wait()
        for l in range(n_list):
            turn_block(kin, kin_t, l, 0.5 if l in (4, 5) else 1.0, clear=l == 4)

        finish_sweep(across_perm, 0)
        launch(across_vert, 1)
        for k in range(1, n_plane):
            shuf_in_copy(shf_hbm, z, k).start()

        def share_end(i):
            @pl.when(by_end)
            def _():
                end_copy(i, sibling).wait_recv()
                for k in range(1, n_chips):
                    end_share_copy(i, chip, lax.rem(chip + k, n_chips)).start()

        def meet_lines():
            @pl.loop(jnp.where(to_high, last - z, 1), n_z - z)
            def _(d):
                pl.semaphore_wait(up.at[d], 1)

            for k in range(1, n_plane):
                t = lax.rem(perm * CORES + core + k, n_plane)
                signal(lines, perm=t // CORES, subj=z * CORES + lax.rem(t, CORES))

        def await_shuf(p):
            for c in range(CORES):
                @pl.when(p * CORES + c != perm * CORES + core)
                def _():
                    await_all(shuf.at[0:n_z], group_recv.at[p * CORES + c])

        def own_tasks(p, first, end):
            @pl.loop(p * n_spans + first, p * n_spans + end)
            def _(task):
                move_own(task)

        def end_tasks(p):
            @pl.loop(0, n_ends)
            def _(turn):
                move_end(p, turn)

        def take_ends():
            @pl.when(by_end)
            def _():
                await_all(end_kin.at[0:(n_chips - 1) * share], peer_recv)
                for l in range(SHARED):
                    turn_block(end_kin, end_t, l, 0.5 if l < 2 else 1.0, clear=l == 0)

            @pl.when(jnp.logical_not(by_end))
            def _():
                end_t[...] = jnp.zeros_like(end_t)

        def square_parts():
            parts[0, 1:2] = square_sum(z * 2 + core)

            @pl.when(by_end)
            def _():
                parts[0, 1:2] += square_sum(near * 2 + core)

            for p in range(1, n_perm):
                parts[p, 1:2] = parts[0, 1:2]

        other_hub = last - z

        def hub_piece(h):
            arrive(other_hub, h, z < 0, subj)

        def near_piece(h):
            arrive(near, h, z > 0, other_hub * CORES + core)

        def far_piece(h):
            arrive(far, h, z < 0, subj)

        plane_rows = CORES * rows
        own_m, own_p = [2 * p for p in range(n_perm)], [2 * p + 1 for p in range(n_perm)]
        end_m, end_p = ([n_half + q for q in part] for part in (own_m, own_p))
        short = last == 3

        turns = [lax.rem(perm + k, n_perm) for k in range(n_perm)]
        event(1, 0, shuf_arrive)
        finish_sweep(across_vert, 1)
        share_end(0)

        @pl.loop(2, last)
        def _(dist):
            event(dist, 0, shuf_arrive)

        own_shuf.wait()
        share_end(1)
        share_end(2)
        await_shuf(turns[0])
        if short:
            own_tasks(turns[0], 0, n_spans // 2)
            near_piece(0)
            hub_piece(0)
            hub_piece(1)
            own_tasks(turns[0], n_spans // 2, n_spans)
            near_piece(1)
            hub_piece(2)
            for turn in turns[1:]:
                await_shuf(turn)
                own_tasks(turn, 0, n_spans // 2)
                near_piece(2)
                hub_piece(3)
                own_tasks(turn, n_spans // 2, n_spans)
            near_piece(3)
            far_piece(0)
            meet_lines()
            take_ends()
            for p in range(n_perm):
                end_tasks(p)
                far_piece(p + 1)
            for q in (z, other_hub, near):
                await_sibling(q)
            square_parts()
            start = (z - 1) * plane_rows
            add(own_m + own_p, start, 3 * plane_rows, first=True)
            for h in range(n_perm + 1, PIECES):
                far_piece(h)
            add(end_p + end_m, start, 3 * plane_rows, first=True)
        else:
            for k, turn in enumerate(turns):
                if k > 0:
                    await_shuf(turn)
                own_tasks(turn, 0, n_spans)

            @pl.loop(1, last)
            def _(dist):
                for h in range(PIECES):
                    event(dist, h, arrive)

            meet_lines()
            await_sibling(z)
            for dist in range(1, last):
                sides(dist, lambda q: await_sibling(q))
            add(own_m + own_p + end_p, plane_rows, (n_z - 2) * plane_rows, first=True)
            take_ends()
            for p in range(n_perm):
                end_tasks(p)
            square_parts()
            add(end_m, plane_rows, (n_z - 2) * plane_rows, first=True)
            add(own_m + own_p + end_p + end_m, near * plane_rows, plane_rows)
        if short:
            await_sibling(far)
        start = far * plane_rows
        for p in range(n_perm):
            cross = 0.0
            for part in range(2):
                q = part * n_half + 2 * p
                left, right = (acc[i] + term(i, start, plane_rows) for i in (q, q + 1))
                cross += jnp.sum(left * right, axis=0, keepdims=True)
            parts[p, 0:1] = cross

        pl.semaphore_wait(lines, n_plane - 1)

        @pl.loop(0, n_all)
        def _(k):
            copy, other = fin_copy(k)
            pl.when(other)(copy.start)

        final[hub_slot(perm, subj)] = parts[perm]

    n_hubs = n_perm * per_hub

    @pl.when(inner)
    def _():
        await_all(final.at[0:n_hubs - 1], fin_recv)

    @pl.when(jnp.logical_not(inner))
    def _():
        await_all(final, fin_recv)

    count = n_subj * rows
    for q in range(n_perm):
        total = jnp.sum(final[q * per_hub:(q + 1) * per_hub], axis=0)
        scale = jnp.sqrt(jnp.float32(count)) * (total[1:2] / count + 1e-05)
        out_ref[:, q * cols:(q + 1) * cols] = 2.0 * total[0:1] / scale

    for way, sending in enumerate((to_low, to_high)):
        @pl.when(sending)
        def _():
            await_sent(gathered.at[0:rows], own_send.at[way])

    @pl.when(inner)
    def _():
        await_sent(shuf.at[0:n_z - 3], shuf_own)
        await_sent(shuf.at[0:n_z * (n_plane - 1)], shuf_in)
        await_sent(gathered.at[0:n_z * rows], sib_send)

        @pl.loop(1, last)
        def _(dist):
            event(dist, 0, drain)

        @pl.when(by_end)
        def _():
            await_sent(end_kin.at[0:(n_chips - 1) * share], end_share)

        await_sent(sent, fin_send)

    @pl.when(jnp.logical_not(inner))
    def _():
        await_sent(shuf.at[0:n_z - 2], shuf_own)
        await_sent(end_kin.at[0:share], end_send)

    @pl.when(z == 0)
    def _():
        pl.semaphore_wait(up.at[last], 1)


def per_device(n_perm, n_subj, n_vert, kinship, phenotype, shuffle):
    rows, width = phenotype.shape
    cols = width // n_perm
    n_all = n_perm * n_subj
    n_z = n_subj // CORES
    n_list = n_z + 3
    n_chips = n_vert * n_perm
    n_hubs = n_perm * (n_subj - 2 * CORES)
    DMA, VMEM = pltpu.SemaphoreType.DMA, pltpu.VMEM
    out = pl.pallas_call(
        functools.partial(kernel, n_perm, n_subj, n_vert),
        out_shape=jax.ShapeDtypeStruct((1, width), jnp.float32),
        in_specs=[pl.BlockSpec(memory_space=pl.ANY)] * 3,
        out_specs=pl.BlockSpec(memory_space=VMEM),
        scratch_shapes=[
            VMEM((rows, n_list * rows), jnp.bfloat16),
            VMEM((rows, SHARED * rows), jnp.bfloat16),
            VMEM((n_list * rows, rows), jnp.bfloat16),
            VMEM((SHARED * rows, rows), jnp.bfloat16),
            VMEM((n_all, 1, rows), jnp.int32),
            VMEM((n_perm * 4, n_subj * rows, rows), jnp.bfloat16),
            VMEM((n_subj * rows, cols), jnp.bfloat16),
            VMEM((n_perm * 4, rows, cols), jnp.float32),
            VMEM((n_perm, 2, cols), jnp.float32),
            VMEM((n_hubs, 2, cols), jnp.float32),
            VMEM((n_all - 1, 2, cols), jnp.float32),
            DMA((3,)),
            pltpu.SemaphoreType.REGULAR((n_z,)), pltpu.SemaphoreType.REGULAR((3,)),
            pltpu.SemaphoreType.REGULAR((2,)), pltpu.SemaphoreType.REGULAR((2,)), pltpu.SemaphoreType.REGULAR,
            DMA((n_z,)), DMA((n_perm * CORES,)), DMA, DMA,
            DMA((n_z, PIECES)), DMA((n_z,)), DMA((2,)), DMA((n_z,)), DMA,
            DMA((SHARED,)), DMA, DMA, DMA, DMA, DMA,
        ],
        compiler_params=pltpu.CompilerParams(collective_id=0, has_side_effects=True),
    )(kinship, phenotype, shuffle.reshape(1, rows))
    return out.reshape(width)


def solution(mesh):
    in_specs = (P("subj", None), P("subj", "vert"), P(("perm", "subj")))
    out_specs = P(("perm", "vert"))
    sizes = [mesh.shape[axis] for axis in ("perm", "subj", "vert")]
    body = functools.partial(per_device, *sizes)
    return jax.shard_map(body, mesh=mesh, in_specs=in_specs, out_specs=out_specs, check_vma=False)
```

```python
import functools

import jax
import jax.numpy as jnp
from jax import lax
from jax.experimental import pallas as pl
from jax.experimental.pallas import tpu as pltpu
from jax.sharding import PartitionSpec as P

MESH = pl.DeviceIdType.MESH
CORES = 2
PIECES = 4
SHARED = 3
SPAN = 4
END_SPAN = 4


def kernel(
    n_perm, n_subj, n_vert,
    kin_hbm, phe_hbm, shf_hbm, out_ref,
    kin, end_kin, kin_t, end_t, shuf, moved, gathered, acc, parts, final, sent,
    load_sem, up, side, across_perm, across_vert, lines,
    line_recv, group_recv, shuf_own, shuf_in,
    row_recv, sib_recv, own_send, row_send, sib_send,
    end_recv, peer_recv, end_send, end_share, fin_send, fin_recv,
):
    perm, subj, vert = lax.axis_index("perm"), lax.axis_index("subj"), lax.axis_index("vert")
    n_all = n_perm * n_subj
    me = perm * n_subj + subj
    z, core = subj // CORES, lax.rem(subj, CORES)
    n_z = n_subj // CORES
    last = n_z - 1
    sibling = z * CORES + (1 - core)
    rows, cols = kin.shape[0], gathered.shape[1]
    piece = rows // PIECES
    n_list = kin.shape[1] // rows
    n_spans = gathered.shape[0] // (SPAN * rows)
    n_plane = n_perm * CORES
    n_chips = n_vert * n_perm
    chip = vert * n_perm + perm
    share = rows // n_chips
    inner = jnp.logical_and(z > 0, z < last)
    by_end = jnp.logical_or(z == 1, z == last - 1)
    first_col = pl.multiple_of(perm * cols, cols)
    barrier = pltpu.get_barrier_semaphore()

    def signal(sem, **device):
        pl.semaphore_signal(sem, inc=1, device_id=device, device_id_type=MESH)

    def half(h):
        return pl.ds(pl.multiple_of(h * piece, piece), piece)

    def spot(q, c, h):
        at = pl.multiple_of((q * CORES + c) * rows + h * piece, piece)
        return gathered.at[pl.ds(at, piece)]

    near = jnp.where(z * 2 < n_z, 0, last)
    far = last - near
    low_end = near == 0
    far_core = jnp.where(low_end, core, 1 - core)

    def listed(l):
        if l == 0:
            return near * CORES + core
        if l == 1:
            return near * CORES + 1 - core
        if l == 2:
            return far * CORES + far_core
        if l == 3:
            return far * CORES + 1 - far_core
        if l == 4:
            return subj
        if l == 5:
            return sibling
        k = l - 5
        other = jnp.where(k < z, k, k + 1)
        return other * CORES + jnp.where(other > z, core, 1 - core)

    def kin_load(l):
        block = pl.multiple_of(listed(l) * rows, rows)
        return pltpu.make_async_copy(
            kin_hbm.at[:, pl.ds(block, rows)], kin.at[:, l * rows:(l + 1) * rows], load_sem.at[0])

    def phe_load(h):
        return pltpu.make_async_copy(
            phe_hbm.at[half(h), pl.ds(first_col, cols)], spot(z, core, h), load_sem.at[1])

    own_shuf = pltpu.make_async_copy(shf_hbm, shuf.at[me], load_sem.at[2])
    loads = [functools.partial(kin_load, l) for l in range(n_list)]
    loads += [functools.partial(phe_load, h) for h in range(PIECES)]

    @pl.loop(z + 1, n_z)
    def _(q):
        signal(barrier, subj=q * CORES + core)

    axes = (
        (perm, n_perm, lambda d: dict(perm=perm + d)),
        (vert, n_vert, lambda d: dict(vert=vert + d)),
        (core, CORES, lambda d: dict(subj=subj + d)),
    )
    for index, size, near_by in axes:
        @pl.when(jnp.logical_and(inner, index < size - 1))
        def _():
            signal(barrier, **near_by(1))

    lower = sum((index > 0).astype(jnp.int32) for index, _, _ in axes)
    lower = z + jnp.where(inner, lower, 0)

    @pl.when(lower > 0)
    def _():
        pl.semaphore_wait(barrier, lower)

    @pl.loop(1, z + 1)
    def _(d):
        signal(up.at[d], subj=subj - CORES * d)

    def answer_plane():
        for i, (index, size, near_by) in enumerate(axes):
            @pl.when(index > 0)
            def _():
                signal(side.at[i], **near_by(-1))

    def meet(i):
        index, size, _ = axes[i]

        @pl.when(index < size - 1)
        def _():
            pl.semaphore_wait(side.at[i], 1)

    def sweep_ways(sem, i):
        index, size, near_by = axes[i]
        up_side, down_side = index < size - 1, index > 0
        return (
            (sem.at[0], lambda done: signal(done, **near_by(1)), down_side, up_side),
            (sem.at[1], lambda done: signal(done, **near_by(-1)), up_side, down_side),
        )

    def launch(sem, i):
        for done, tell, behind, ahead in sweep_ways(sem, i):
            pl.when(jnp.logical_and(ahead, jnp.logical_not(behind)))(functools.partial(tell, done))

    def finish_sweep(sem, i):
        for done, tell, behind, ahead in sweep_ways(sem, i):
            @pl.when(behind)
            def _():
                pl.semaphore_wait(done, 1)
                pl.when(ahead)(functools.partial(tell, done))

    def remote(src, dst, send, recv, **device):
        return pltpu.make_async_remote_copy(
            src_ref=src, dst_ref=dst, send_sem=send, recv_sem=recv, device_id=device, device_id_type=MESH)

    def await_sent(ref, sem):
        remote(ref, ref, sem, sem, subj=sibling).wait_send()

    def await_all(ref, sem):
        remote(ref, ref, sem, sem, subj=sibling).wait_recv()

    def own_copy(h, way, target):
        return remote(
            phe_hbm.at[half(h), pl.ds(first_col, cols)], spot(z, core, h),
            own_send.at[way], row_recv.at[z, h], subj=target)

    def own_sib_copy(h):
        return remote(
            phe_hbm.at[half(h), pl.ds(first_col, cols)], spot(z, core, h), sib_send, sib_recv.at[z], subj=sibling)

    def pass_copy(q, h, target):
        here = spot(q, core, h)
        return remote(here, here, row_send.at[q], row_recv.at[q, h], subj=target)

    def sib_copy(q, h):
        here = spot(q, core, h)
        return remote(here, here, sib_send, sib_recv.at[q], subj=sibling)

    def shuf_own_copy(q):
        return remote(shf_hbm, shuf.at[me], shuf_own, line_recv.at[z], subj=q * CORES + core)

    def shuf_in_copy(src, q, k):
        t = lax.rem(perm * CORES + core + k, n_plane)
        slot = perm * n_subj + q * CORES + core
        return remote(src, shuf.at[slot], shuf_in, group_recv.at[perm * CORES + core],
                      perm=t // CORES, subj=z * CORES + lax.rem(t, CORES))

    def part_of(owner):
        return pl.ds(pl.multiple_of(owner * share, share), share)

    def end_block(i):
        end_core = core if i == 0 else 1 - core
        if i < 2:
            return z * CORES + end_core
        return jnp.where(z == 0, last * CORES + core, 1 - core)

    def end_copy(i, target):
        block = pl.multiple_of(end_block(i) * rows, rows)
        return remote(
            kin_hbm.at[part_of(chip), pl.ds(block, rows)], end_kin.at[part_of(chip), i * rows:(i + 1) * rows],
            end_send, end_recv.at[i], subj=target)

    def end_share_copy(i, owner, t):
        here = end_kin.at[part_of(owner), i * rows:(i + 1) * rows]
        return remote(here, here, end_share, peer_recv, vert=t // n_perm, perm=lax.rem(t, n_perm))

    def send_ends(target):
        @pl.when(jnp.logical_not(inner))
        def _():
            for i in range(SHARED):
                end_copy(i, target).start()

    def send_rows(way, target):
        for h in range(PIECES):
            own_copy(h, way, target).start()

    to_low, to_high = z >= 2, z <= last - 2

    pl.when(inner)(answer_plane)

    @pl.when(to_low)
    def _():
        @pl.loop(1, z)
        def _(k):
            shuf_own_copy(z - k).start()

        send_ends(subj - CORES)
        send_rows(0, subj - CORES)

    @pl.when(inner)
    def _():
        for load in loads:
            load().start()
        own_shuf.start()

    @pl.when(to_high)
    def _():
        pl.semaphore_wait(up.at[1], 1)
        shuf_own_copy(z + 1).start()
        send_ends(subj + CORES)

        @pl.loop(2, last - z)
        def _(d):
            pl.semaphore_wait(up.at[d], 1)
            shuf_own_copy(z + d).start()

        send_rows(1, subj + CORES)

    def event(dist, h, act):
        @pl.when(z + dist < n_z)
        def _():
            act(z + dist, h, z > 1, subj - CORES)

        @pl.when(z - dist >= 0)
        def _():
            act(z - dist, h, z < last - 1, subj + CORES)

    def arrive(q, h, onward, target):
        pass_copy(q, h, sibling).wait_recv()

        @pl.when(onward)
        def _():
            pass_copy(q, h, target).start()

        sib_copy(q, h).start()

    def drain(q, h, onward, target):
        @pl.when(onward)
        def _():
            await_sent(gathered.at[0:rows], row_send.at[q])

    def shuf_arrive(q, h, onward, target):
        slot = perm * n_subj + q * CORES + core
        await_all(shuf.at[slot], line_recv.at[q])
        for k in range(1, n_plane):
            shuf_in_copy(shuf.at[slot], q, k).start()

    def picks_of(p, first, span, l):
        subject = lax.broadcasted_iota(jnp.int32, (span, rows), 0) + first
        return (subject == shuf[p * n_subj + listed(l)]).astype(jnp.bfloat16)

    span, end_span = SPAN * rows, END_SPAN * rows
    n_ends = gathered.shape[0] // end_span

    def move_own(task):
        p, turn = task // n_spans, lax.rem(task, n_spans)
        picks = [picks_of(p, turn * span, span, l) for l in range(n_list)]
        out = jnp.dot(jnp.concatenate(picks, axis=1), kin_t[...], preferred_element_type=jnp.float32)
        at = pl.ds(pl.multiple_of(turn * span, span), span)
        moved[2 * p, at] = out.astype(jnp.bfloat16)
        moved[2 * p + 1, at] = picks[4]
        moved[2 * (n_perm + p) + 1, at] = picks[0]

    def move_end(p, turn):
        picks = [picks_of(p, turn * end_span, end_span, l) for l in range(SHARED)]
        out = jnp.dot(jnp.concatenate(picks, axis=1), end_t[...], preferred_element_type=jnp.float32)
        at = pl.ds(pl.multiple_of(turn * end_span, end_span), end_span)
        moved[2 * (n_perm + p), at] = out.astype(jnp.bfloat16)

    n_half = n_perm * 2

    def term(q, start, length):
        at = pl.ds(pl.multiple_of(start, rows), length)
        return lax.dot_general(
            moved[q, at], gathered[at], (((0,), (0,)), ((), ())), preferred_element_type=jnp.float32)

    def add(which, start, length, first=False):
        for q in which:
            new = term(q, start, length)
            acc[q] = new if first else acc[q] + new

    def sides(dist, act):
        @pl.loop(0, 2)
        def _(side):
            q = z + dist * (1 - 2 * side)

            @pl.when(jnp.logical_and(q >= 0, q < n_z))
            def _():
                act(q)

    def await_sibling(q):
        await_all(gathered.at[0:rows], sib_recv.at[q])

    def turn_block(src, dst, l, scale, clear=False):
        block = jnp.transpose(src[:, l * rows:(l + 1) * rows].astype(jnp.float32)) * scale
        if clear:
            down = lax.broadcasted_iota(jnp.int32, (rows, rows), 0)
            across = lax.broadcasted_iota(jnp.int32, (rows, rows), 1)
            block = jnp.where(down == across, 0.0, block)
        dst[l * rows:(l + 1) * rows] = block.astype(jnp.bfloat16)

    def square_sum(chunk):
        own = gathered[pl.ds(pl.multiple_of(chunk * rows, rows), rows)].astype(jnp.float32)
        return jnp.sum(own * own, axis=0, keepdims=True)


    per_hub = n_subj - 2 * CORES

    def hub_slot(p, s):
        return p * per_hub + s - CORES

    def send_parts(p):
        @pl.loop(0, n_subj)
        def _(s):
            @pl.when(p * n_subj + s != me)
            def _():
                mine = final.at[hub_slot(perm, subj)]
                remote(parts.at[p], mine, fin_send, fin_recv, perm=p, subj=s).start()

    @pl.when(inner)
    def _():
        meet(2)
        for h in range(PIECES):
            own_sib_copy(h).start()
        meet(0)
        launch(across_perm, 0)
        meet(1)
        pltpu.make_async_copy(kin, kin, load_sem.at[0]).wait()
        pltpu.make_async_copy(gathered.at[0:rows], gathered.at[0:rows], load_sem.at[1]).wait()
        for l in range(n_list):
            turn_block(kin, kin_t, l, 0.5 if l in (4, 5) else 1.0, clear=l == 4)

        finish_sweep(across_perm, 0)
        launch(across_vert, 1)
        for k in range(1, n_plane):
            shuf_in_copy(shf_hbm, z, k).start()

        def share_end(i):
            @pl.when(by_end)
            def _():
                end_copy(i, sibling).wait_recv()
                for k in range(1, n_chips):
                    end_share_copy(i, chip, lax.rem(chip + k, n_chips)).start()

        def meet_lines():
            @pl.loop(jnp.where(to_high, last - z, 1), n_z - z)
            def _(d):
                pl.semaphore_wait(up.at[d], 1)

            for k in range(1, n_plane):
                t = lax.rem(perm * CORES + core + k, n_plane)
                signal(lines, perm=t // CORES, subj=z * CORES + lax.rem(t, CORES))

        def await_shuf(p):
            for c in range(CORES):
                @pl.when(p * CORES + c != perm * CORES + core)
                def _():
                    await_all(shuf.at[0:n_z], group_recv.at[p * CORES + c])

        def own_tasks(p, first, end):
            @pl.loop(p * n_spans + first, p * n_spans + end)
            def _(task):
                move_own(task)

        def end_tasks(p):
            @pl.loop(0, n_ends)
            def _(turn):
                move_end(p, turn)

        def take_ends():
            @pl.when(by_end)
            def _():
                await_all(end_kin.at[0:(n_chips - 1) * share], peer_recv)
                for l in range(SHARED):
                    turn_block(end_kin, end_t, l, 0.5 if l < 2 else 1.0, clear=l == 0)

            @pl.when(jnp.logical_not(by_end))
            def _():
                end_t[...] = jnp.zeros_like(end_t)

        def square_parts():
            parts[0, 1:2] = square_sum(z * 2 + core)

            @pl.when(by_end)
            def _():
                parts[0, 1:2] += square_sum(near * 2 + core)

            for p in range(1, n_perm):
                parts[p, 1:2] = parts[0, 1:2]

        other_hub = last - z

        def hub_piece(h):
            arrive(other_hub, h, z < 0, subj)

        def near_piece(h):
            arrive(near, h, z > 0, other_hub * CORES + core)

        def far_piece(h):
            arrive(far, h, z < 0, subj)

        plane_rows = CORES * rows
        own_m, own_p = [2 * p for p in range(n_perm)], [2 * p + 1 for p in range(n_perm)]
        end_m, end_p = ([n_half + q for q in part] for part in (own_m, own_p))
        short = last == 3

        turns = [lax.rem(perm + k, n_perm) for k in range(n_perm)]
        event(1, 0, shuf_arrive)
        finish_sweep(across_vert, 1)
        share_end(0)

        @pl.loop(2, last)
        def _(dist):
            event(dist, 0, shuf_arrive)

        own_shuf.wait()
        share_end(1)
        share_end(2)
        await_shuf(turns[0])
        if short:
            own_tasks(turns[0], 0, n_spans // 2)
            near_piece(0)
            hub_piece(0)
            hub_piece(1)
            own_tasks(turns[0], n_spans // 2, n_spans)
            near_piece(1)
            hub_piece(2)
            for turn in turns[1:]:
                await_shuf(turn)
                own_tasks(turn, 0, n_spans // 2)
                near_piece(2)
                hub_piece(3)
                own_tasks(turn, n_spans // 2, n_spans)
            near_piece(3)
            far_piece(0)
            meet_lines()
            take_ends()
            for p in range(n_perm):
                end_tasks(p)
                far_piece(p + 1)
            for q in (z, other_hub, near):
                await_sibling(q)
            square_parts()
            start = (z - 1) * plane_rows
            add(own_m + own_p, start, 3 * plane_rows, first=True)
            for h in range(n_perm + 1, PIECES):
                far_piece(h)
            add(end_p + end_m, start, 3 * plane_rows, first=True)
        else:
            for k, turn in enumerate(turns):
                if k > 0:
                    await_shuf(turn)
                own_tasks(turn, 0, n_spans)

            @pl.loop(1, last)
            def _(dist):
                for h in range(PIECES):
                    event(dist, h, arrive)

            meet_lines()
            await_sibling(z)
            for dist in range(1, last):
                sides(dist, lambda q: await_sibling(q))
            add(own_m + own_p + end_p, plane_rows, (n_z - 2) * plane_rows, first=True)
            take_ends()
            for p in range(n_perm):
                end_tasks(p)
            square_parts()
            add(end_m, plane_rows, (n_z - 2) * plane_rows, first=True)
            add(own_m + own_p + end_p + end_m, near * plane_rows, plane_rows)
        if short:
            await_sibling(far)
        pl.semaphore_wait(lines, n_plane - 1)
        start = far * plane_rows
        for p in range(n_perm):
            cross = 0.0
            for part in range(2):
                q = part * n_half + 2 * p
                left, right = (acc[i] + term(i, start, plane_rows) for i in (q, q + 1))
                cross += jnp.sum(left * right, axis=0, keepdims=True)
            parts[p, 0:1] = cross
            send_parts(p)

        final[hub_slot(perm, subj)] = parts[perm]

    n_hubs = n_perm * per_hub

    @pl.when(inner)
    def _():
        await_all(final.at[0:n_hubs - 1], fin_recv)

    @pl.when(jnp.logical_not(inner))
    def _():
        await_all(final, fin_recv)

    count = n_subj * rows
    for q in range(n_perm):
        total = jnp.sum(final[q * per_hub:(q + 1) * per_hub], axis=0)
        scale = jnp.sqrt(jnp.float32(count)) * (total[1:2] / count + 1e-05)
        out_ref[:, q * cols:(q + 1) * cols] = 2.0 * total[0:1] / scale

    for way, sending in enumerate((to_low, to_high)):
        @pl.when(sending)
        def _():
            await_sent(gathered.at[0:rows], own_send.at[way])

    @pl.when(inner)
    def _():
        await_sent(shuf.at[0:n_z - 3], shuf_own)
        await_sent(shuf.at[0:n_z * (n_plane - 1)], shuf_in)
        await_sent(gathered.at[0:n_z * rows], sib_send)

        @pl.loop(1, last)
        def _(dist):
            event(dist, 0, drain)

        @pl.when(by_end)
        def _():
            await_sent(end_kin.at[0:(n_chips - 1) * share], end_share)

        await_sent(sent, fin_send)

    @pl.when(jnp.logical_not(inner))
    def _():
        await_sent(shuf.at[0:n_z - 2], shuf_own)
        await_sent(end_kin.at[0:share], end_send)

    @pl.when(z == 0)
    def _():
        pl.semaphore_wait(up.at[last], 1)


def per_device(n_perm, n_subj, n_vert, kinship, phenotype, shuffle):
    rows, width = phenotype.shape
    cols = width // n_perm
    n_all = n_perm * n_subj
    n_z = n_subj // CORES
    n_list = n_z + 3
    n_chips = n_vert * n_perm
    n_hubs = n_perm * (n_subj - 2 * CORES)
    DMA, VMEM = pltpu.SemaphoreType.DMA, pltpu.VMEM
    out = pl.pallas_call(
        functools.partial(kernel, n_perm, n_subj, n_vert),
        out_shape=jax.ShapeDtypeStruct((1, width), jnp.float32),
        in_specs=[pl.BlockSpec(memory_space=pl.ANY)] * 3,
        out_specs=pl.BlockSpec(memory_space=VMEM),
        scratch_shapes=[
            VMEM((rows, n_list * rows), jnp.bfloat16),
            VMEM((rows, SHARED * rows), jnp.bfloat16),
            VMEM((n_list * rows, rows), jnp.bfloat16),
            VMEM((SHARED * rows, rows), jnp.bfloat16),
            VMEM((n_all, 1, rows), jnp.int32),
            VMEM((n_perm * 4, n_subj * rows, rows), jnp.bfloat16),
            VMEM((n_subj * rows, cols), jnp.bfloat16),
            VMEM((n_perm * 4, rows, cols), jnp.float32),
            VMEM((n_perm, 2, cols), jnp.float32),
            VMEM((n_hubs, 2, cols), jnp.float32),
            VMEM((n_all - 1, 2, cols), jnp.float32),
            DMA((3,)),
            pltpu.SemaphoreType.REGULAR((n_z,)), pltpu.SemaphoreType.REGULAR((3,)),
            pltpu.SemaphoreType.REGULAR((2,)), pltpu.SemaphoreType.REGULAR((2,)), pltpu.SemaphoreType.REGULAR,
            DMA((n_z,)), DMA((n_perm * CORES,)), DMA, DMA,
            DMA((n_z, PIECES)), DMA((n_z,)), DMA((2,)), DMA((n_z,)), DMA,
            DMA((SHARED,)), DMA, DMA, DMA, DMA, DMA,
        ],
        compiler_params=pltpu.CompilerParams(collective_id=0, has_side_effects=True),
    )(kinship, phenotype, shuffle.reshape(1, rows))
    return out.reshape(width)


def solution(mesh):
    in_specs = (P("subj", None), P("subj", "vert"), P(("perm", "subj")))
    out_specs = P(("perm", "vert"))
    sizes = [mesh.shape[axis] for axis in ("perm", "subj", "vert")]
    body = functools.partial(per_device, *sizes)
    return jax.shard_map(body, mesh=mesh, in_specs=in_specs, out_specs=out_specs, check_vma=False)
```
